128 devices in a mesh: row: 16 (over z, y), col: 8 (over x, core).
Axes of the slice: x: 4, y: 4, z: 4, core: 2. Of those that a mesh axis runs over, the one named last changes fastest.
Arguments:
- features: float32 [16384, 128], P(('row', 'col')), may hold values from -6 to 6
- noise: float32 [16384], P(('row', 'col')), may hold values from 0.05 to 0.5
- owner_slot: int32 [16384], P(('row', 'col')), may hold values from 0 to 16383, as said below
- inv_length: float32 [128], replicated, may hold values from 0.001953125 to 0.03125
Outputs:
- factored: bfloat16 [16384, 16384], P('row', 'col')
The draws below stay inside these ranges and needn't reach their ends.
Inputs may be any that keep to these rules, and one draw needn't show every extreme that they name: `owner_slot`: A permutation of the storage rows. Storage rows are split into 128 ranges of 128 in order; the 128 samples of range e go to the ranges with the same remainder modulo 8, exactly 8 of them to each such range.
All inputs are finite; a program needn't handle non-finite values.
Results may differ from the reference program's by a relative error of at most 0.0082.
Values may be sent and summed in bfloat16 or wider, within the bound.
No kernel may reach another device: no remote copies, remote signals or barrier semaphores. Data moves between devices by JAX's collectives and lax.ppermute only.
A program may use at most 128 MiB of HBM per device.

```python
import math
import jax
import jax.numpy as jnp
from jax import lax

F = 128
NB = 512
PANELS = 2
RB = 2
M = 16384
SPD = 128
PER = 8
N_ROW = 16
N_COL = 8


def draw_owner_slot(key, part):
    halves = jax.random.split(key, 2)
    send_keys = jax.random.split(halves[0], N_ROW * N_COL)
    take_keys = jax.random.split(halves[1], N_ROW * N_COL)
    send_order = jax.vmap(lambda single: jax.random.permutation(single, SPD))(send_keys).reshape(N_ROW, N_COL, SPD)
    take_order = jax.vmap(lambda single: jax.random.permutation(single, SPD))(take_keys).reshape(N_ROW, N_COL, SPD)
    shape = (N_ROW, N_ROW, N_COL, PER)
    source_row = lax_iota(shape, 0)
    target_row = lax_iota(shape, 1)
    column = lax_iota(shape, 2)
    within = lax_iota(shape, 3)
    source = (source_row * N_COL + column) * SPD + send_order[source_row, column, target_row * PER + within]
    target = (target_row * N_COL + column) * SPD + take_order[target_row, column, source_row * PER + within]
    result = jnp.zeros((M,), jnp.int32).at[source.reshape(-1)].set(target.reshape(-1).astype(jnp.int32))
    return result


def lax_iota(shape, dimension):
    return jax.lax.broadcasted_iota(jnp.int32, shape, dimension)


def level_of(own_key, extent, cuts, smallest, top_value):
    gain, own = 1.0, jax.random.fold_in(own_key, 6)
    for dim, shards_of in cuts:
        heights = jnp.exp(jax.random.uniform(jax.random.fold_in(own, dim), (shards_of,), jnp.float32, smallest / len(cuts), top_value / len(cuts)))
        gain = gain * jnp.repeat(heights, extent[dim] // shards_of).reshape([-1 if axis == dim else 1 for axis in range(len(extent))])
    return gain


def normal_values(stream_key, shape, spread, reach, cuts=(), kind=jnp.bfloat16):
    values = spread * jax.random.normal(stream_key, shape, jnp.float32)
    if cuts:
        values = values * level_of(stream_key, shape, cuts, -0.22, 0.18)
    return jnp.clip(values, -reach, reach).astype(kind)


def setup_inputs(seed: int = 0) -> dict:
    splits = jax.random.split(jax.random.key(seed), 5)
    features = normal_values(splits[0], (M, F), 1.0, 6.0, ((0, 128),), jnp.float32)
    noise = jnp.clip(jnp.exp(math.log(0.5) - 2.3025851 * jax.random.uniform(splits[1], (M,), jnp.float32) ** level_of(splits[1], (M,), ((0, 128),), -0.2, 0.2)), 0.05, 0.5)
    owner_slot = draw_owner_slot(jax.random.fold_in(splits[4], 71), 0)
    inv_length = jnp.clip(jnp.exp(jax.random.uniform(splits[3], (F,), jnp.float32, math.log(0.001953125), math.log(0.03125))), 0.001953125, 0.03125)
    return dict(features=features, noise=noise, owner_slot=owner_slot, inv_length=inv_length)


def kernel_block(left, right, scale):
    left_sq = jnp.sum(left * left * scale, axis=1)
    right_sq = jnp.sum(right * right * scale, axis=1)
    cross = jnp.einsum('rf,cf->rc', left * scale, right, precision=lax.Precision.HIGHEST)
    return jnp.exp(-0.5 * (left_sq[:, None] + right_sq[None, :] - 2.0 * cross))

def reference(features, noise, owner_slot, inv_length):
    rounded = lax.optimization_barrier(features.astype(jnp.bfloat16)).astype(jnp.float32)
    noise_round = lax.optimization_barrier(noise.astype(jnp.bfloat16)).astype(jnp.float32)
    slots = owner_slot.astype(jnp.int32)
    stored = jnp.zeros((M, F), jnp.float32).at[slots].set(rounded)
    stored_noise = jnp.zeros((M,), jnp.float32).at[slots].set(noise_round)
    ordered = stored.reshape(N_ROW, RB, NB, F).transpose(1, 0, 2, 3).reshape(M, F)
    ordered_noise = stored_noise.reshape(N_ROW, RB, NB).transpose(1, 0, 2).reshape(M)
    width = PANELS * NB
    position = jnp.arange(M, dtype=jnp.int32)
    leading = kernel_block(ordered, ordered[:width], inv_length)
    leading = leading + jnp.where(position[:, None] == position[None, :width], ordered_noise[:, None], 0.0)
    panels = jnp.zeros((M, 0), jnp.bfloat16)
    for panel_index in range(PANELS):
        lower = panel_index * NB
        column = leading[:, lower:lower + NB] - jnp.dot(panels.astype(jnp.float32), panels[lower:lower + NB].T.astype(jnp.float32), preferred_element_type=jnp.float32)
        factor = jnp.linalg.cholesky(column[lower:lower + NB])
        inverse = jax.scipy.linalg.solve_triangular(factor, jnp.eye(NB, dtype=jnp.float32), lower=True)
        panel = jnp.dot(column.astype(jnp.float32), inverse.T.astype(jnp.float32), precision=lax.Precision.HIGHEST, preferred_element_type=jnp.float32)
        panel = jnp.where(position[:, None] >= lower, panel, 0.0).astype(jnp.bfloat16)
        panels = jnp.concatenate([panels, panel], axis=1)

    def one_block(start):
        block_rows = lax.dynamic_slice_in_dim(ordered, start, NB, 0)
        block_noise = lax.dynamic_slice_in_dim(ordered_noise, start, NB, 0)
        block_panel = lax.dynamic_slice_in_dim(panels, start, NB, 0)
        global_rows = start + jnp.arange(NB, dtype=jnp.int32)
        block = kernel_block(block_rows, ordered, inv_length)
        block = block + jnp.where(global_rows[:, None] == position[None, :], block_noise[:, None], 0.0)
        block = block - jnp.dot(block_panel.astype(jnp.float32), panels.T.astype(jnp.float32), preferred_element_type=jnp.float32)
        keep = (global_rows[:, None] >= width) & (position[None, :] >= width)
        block = jnp.where(keep, block, 0.0)
        block = jnp.where(position[None, :] < width, jnp.pad(block_panel.astype(jnp.float32), ((0, 0), (0, M - width))), block)
        return block.astype(jnp.bfloat16)
    starts = jnp.arange(M // NB, dtype=jnp.int32) * NB
    whole = lax.map(one_block, starts).reshape(M, M)
    whole = whole.reshape(RB, N_ROW, NB, M).transpose(1, 0, 2, 3).reshape(M, M)
    col_blocks = M // (N_COL * NB)
    whole = whole.reshape(M, col_blocks, N_COL, NB).transpose(0, 2, 1, 3).reshape(M, M)
    return whole
```

```python
import jax
import jax.numpy as jnp
from jax import lax
from jax.experimental import pallas as pl
from jax.experimental.pallas import tpu as pltpu
from jax.sharding import PartitionSpec as P

NB = 512
PANELS = 2
F = 128
f32 = jnp.float32
bf16 = jnp.bfloat16


def split3(x):
    h = x.astype(bf16)
    r = x - h.astype(f32)
    m = r.astype(bf16)
    return h, m, (r - m.astype(f32)).astype(bf16)


def left6(pieces):
    h, m, l = pieces
    return jnp.concatenate([h, h, m, m, h, l], axis=1)


def right6(pieces, axis):
    h, m, l = pieces
    return jnp.concatenate([h, m, h, m, l, h], axis=axis)


def nt(x, y):
    return lax.dot_general(x, y, (((1,), (1,)), ((), ())), preferred_element_type=f32)


def nn(x, y):
    return lax.dot_general(x, y, (((1,), (0,)), ((), ())), preferred_element_type=f32)


def iota(shape, dim):
    return lax.broadcasted_iota(jnp.int32, shape, dim)


def pack_kernel(feat_ref, noise_ref, slot_col_ref, slot_row_ref, sorted_ref, extra_ref):
    n = feat_ref.shape[0]
    col = slot_col_ref[...]
    row = slot_row_ref[...]
    before = (row < col).astype(f32)
    rank_col = jnp.sum(before, axis=1, keepdims=True).astype(jnp.int32)
    rank_row = jnp.sum((col < row).astype(f32), axis=0, keepdims=True).astype(jnp.int32)
    pick = (iota((n, n), 0) == rank_row).astype(bf16)
    sorted_ref[...] = nn(pick, feat_ref[...].astype(bf16)).astype(bf16)
    back = rank_col == iota((n, n), 1)
    slots = jnp.sum(jnp.where(back, (col % n).astype(f32), 0.0), axis=0, keepdims=True)
    noises = jnp.sum(
        jnp.where(back, noise_ref[...].astype(bf16).astype(f32), 0.0), axis=0, keepdims=True
    )
    which = iota((8, n), 0)
    extra_ref[...] = jnp.where(which == 0, slots, jnp.where(which == 1, noises, 0.0)).astype(bf16)


def spread_rows(table, target):
    n = table.shape[0]
    lane = iota((n, n), 1)
    mine = jnp.where(lane // 8 == target, table, jnp.zeros_like(table))
    comb = (iota((n, n), 0) % 8 == iota((n, n), 1) % 8).astype(bf16)
    spread = nn(mine, comb).reshape(n // 8, 8, n)
    take = iota((n // 8, 8, n), 2) // 8 == iota((n // 8, 8, n), 0)
    return jnp.sum(jnp.where(take, spread, 0.0), axis=0)


def place_range(slots, noises, samples):
    n = samples.shape[0]
    hot = iota((n, n), 0).astype(f32) == slots
    rows = nn(hot.astype(bf16), samples).astype(bf16)
    noise = jnp.sum(jnp.where(hot, noises, 0.0), axis=1, keepdims=True)
    return rows, noise


def fill_lanes(values, width):
    lane = iota((values[0].shape[0], width), 1)
    out = jnp.zeros((values[0].shape[0], width), f32)
    for i, v in enumerate(values):
        out = jnp.where(lane == i, v, out)
    return out.astype(bf16)


def half_norm(x, scale):
    return -0.5 * jnp.sum(x * x * scale, axis=1, keepdims=True)


def left_operand(rows, scale):
    h, m, l = split3(half_norm(rows.astype(f32), scale))
    extra = fill_lanes([1.0 + 0.0 * h.astype(f32)] * 3 + [h.astype(f32), m.astype(f32), l.astype(f32)], F)
    return jnp.concatenate([rows, rows, rows, extra], axis=1)


def right_operand(rows, scale):
    x = rows.astype(f32)
    h, m, l = split3(half_norm(x, scale))
    extra = fill_lanes([h.astype(f32), m.astype(f32), l.astype(f32)] + [1.0 + 0.0 * h.astype(f32)] * 3, F)
    return jnp.concatenate([*split3(x * scale), extra], axis=1)


def add_diagonal(value, noise):
    n = value.shape[0]
    return value + jnp.where(iota((n, n), 0) == iota((n, n), 1), noise, 0.0)


def lane(x, j):
    return jnp.broadcast_to(x[:, j : j + 1], (8, 128))


def sub(x, k):
    return jnp.broadcast_to(x[k : k + 1, :], (8, 128))


def invert_factor(block):
    ri = iota((8, 128), 0)
    ci = iota((8, 128), 1)
    a = [block[8 * i : 8 * i + 8, :] for i in range(16)]
    b = [(ri + 8 * i == ci).astype(f32) for i in range(16)]
    out = []
    for g in range(16):
        cb = [lane(a[g], 8 * g + k) for k in range(8)]
        d = [[sub(cb[k], r) if r >= k else None for k in range(8)] for r in range(8)]
        ar = [sub(a[g], k) for k in range(8)]
        br = [sub(b[g], k) for k in range(8)]
        more = g + 1 < 16
        cc = [lane(a[g + 1], 8 * g + k) for k in range(8)] if more else None
        rs = [None] * 8
        l = [[None] * 8 for _ in range(8)]
        for k in range(8):
            rs[k] = lax.rsqrt(d[k][k])
            for m in range(k + 1, 8):
                l[m][k] = d[m][k] * rs[k]
            for m in range(k + 1, 8):
                for j in range(k + 1, m + 1):
                    d[m][j] = d[m][j] - l[m][k] * l[j][k]
            ar[k] = ar[k] * rs[k]
            br[k] = br[k] * rs[k]
            if more:
                cc[k] = cc[k] * rs[k]
            for m in range(k + 1, 8):
                ar[m] = ar[m] - l[m][k] * ar[k]
                br[m] = br[m] - l[m][k] * br[k]
                if more:
                    cc[m] = cc[m] - l[m][k] * cc[k]
            if more:
                a[g + 1] = a[g + 1] - cc[k] * ar[k]
                b[g + 1] = b[g + 1] - cc[k] * br[k]
        v = br[7]
        for k in range(7):
            v = jnp.where(ri == k, br[k], v)
        out.append(v)
        if g + 2 < 16:
            z = [None] * 8
            y = [None] * 8
            for k in range(7, -1, -1):
                zz = ar[k]
                yy = br[k]
                for m in range(7, k, -1):
                    zz = zz - l[m][k] * z[m]
                    yy = yy - l[m][k] * y[m]
                z[k] = zz * rs[k]
                y[k] = yy * rs[k]
            for i in range(g + 2, 16):
                ai = a[i]
                bi = b[i]
                for k in range(8):
                    c = lane(a[i], 8 * g + k)
                    ai = ai - c * z[k]
                    bi = bi - c * y[k]
                a[i] = ai
                b[i] = bi
    return jnp.concatenate(out, axis=0)


def invert_panel(a_ref, w_ref):
    w_ref[...] = jnp.zeros((NB, NB), f32)
    for s in range(0, NB, 128):
        e = s + 128
        w = invert_factor(a_ref[s:e, s:e])
        pieces = split3(w)
        wl = left6(pieces)
        if e < NB:
            low = nt(left6(split3(a_ref[e:NB, s:e])), right6(pieces, 1))
            low_pieces = split3(low)
            low_left = left6(low_pieces)
            a_ref[e:NB, e:NB] = a_ref[e:NB, e:NB] - nt(low_left, right6(low_pieces, 1))
        if s > 0:
            w_ref[s:e, 0:s] = nn(wl, right6(split3(w_ref[s:e, 0:s]), 0))
        w_ref[s:e, s:e] = w
        if e < NB:
            w_ref[e:NB, 0:e] = w_ref[e:NB, 0:e] - nn(low_left, right6(split3(w_ref[s:e, 0:e]), 0))


def times_inverse(left, pieces):
    half = NB // 2
    lp = split3(left)
    top = nt(
        left6([p[:, :half] for p in lp]), right6([p[:half, :half] for p in pieces], 1)
    )
    bottom = nt(left6(lp), right6([p[half:, :] for p in pieces], 1))
    return jnp.concatenate([top, bottom], axis=1)


def factor_kernel(
    place_ref, samples_ref, slot_ref, noise_ref, scale_ref,
    right_ref, lead_noise_ref, w_ref, p21_ref, slots_ref, noises_ref, a_ref, inv_ref,
):
    scale = scale_ref[...]
    slot_table = slot_ref[...]
    noise_table = noise_ref[...]
    for panel in range(PANELS):
        slots = spread_rows(slot_table, panel)
        noises = spread_rows(noise_table, panel)
        rows = []
        for i in range(4):
            placed, noise = place_range(
                slots[i : i + 1, :], noises[i : i + 1, :], samples_ref[panel * 4 + i]
            )
            rows.append(placed)
            lead_noise_ref[panel * NB + i * 128 : panel * NB + (i + 1) * 128, :] = noise
        rows = jnp.concatenate(rows, axis=0)
        right_ref[panel * NB : (panel + 1) * NB, :] = right_operand(rows, scale)
        left = left_operand(rows, scale)
        for other in range(panel + 1):
            value = jnp.exp(nt(left, right_ref[other * NB : (other + 1) * NB, :]))
            if other == panel:
                value = add_diagonal(value, lead_noise_ref[panel * NB : (panel + 1) * NB, :])
            a_ref[panel + other] = value

    for kind in range(3):
        slots_ref[kind] = spread_rows(slot_table, place_ref[kind])
        noises_ref[kind] = spread_rows(noise_table, place_ref[kind])

    def one_panel(panel, carry):
        invert_panel(a_ref.at[0], inv_ref)
        pieces = split3(inv_ref[...])
        for i in range(3):
            w_ref[panel, i] = pieces[i]

        @pl.when(panel == 0)
        def _():
            p21 = times_inverse(a_ref[1], pieces).astype(bf16)
            p21_ref[...] = p21
            a_ref[0] = a_ref[2] - nt(p21, p21)

        return carry

    lax.fori_loop(0, PANELS, one_panel, 0)


def panel_kernel(
    block_ref, samples_ref, slots_ref, noises_ref, scale_ref, right_ref, lead_noise_ref,
    w_ref, p21_ref, rows_ref, noise_ref, p_ref,
):
    step = pl.program_id(0)
    kind = jnp.where(step < 2, 0, 1 + step % 2)
    first = 4 * jnp.where(step < 2, step, (step - 2) // 2)
    block = block_ref[step]
    rows = []
    for i in range(4):
        placed, noise = place_range(
            slots_ref[kind, pl.ds(first + i, 1), :],
            noises_ref[kind, pl.ds(first + i, 1), :],
            samples_ref[0, i],
        )
        rows.append(placed)
        noise_ref[i * 128 : (i + 1) * 128, :] = noise
    rows = jnp.concatenate(rows, axis=0)
    rows_ref[...] = rows
    left = left_operand(rows, scale_ref[...])
    columns = []
    for panel in range(PANELS):
        value = jnp.exp(nt(left, right_ref[panel * NB : (panel + 1) * NB, :]))
        lead = jnp.where(block == panel, lead_noise_ref[panel * NB : (panel + 1) * NB, :], 0.0)
        columns.append(add_diagonal(value, lead))
    p1 = times_inverse(columns[0], [w_ref[0, i] for i in range(3)]).astype(bf16)
    p_ref[:, :NB] = p1
    second = columns[1] - nt(p1, p21_ref[...])
    p2 = times_inverse(second, [w_ref[1, i] for i in range(3)])
    p_ref[:, NB:] = jnp.where(block >= 1, p2, 0.0).astype(bf16)


def tile_kernel(
    block_ref, left_rows_ref, right_rows_ref, noise_ref, scale_ref, p_left_ref, p_right_ref,
    out_ref, right_ref,
):
    row_block = block_ref[pl.program_id(1)]
    col_block = block_ref[2 + pl.program_id(0)]

    @pl.when(pl.program_id(1) == 0)
    def _():
        right_ref[...] = right_operand(right_rows_ref[...], scale_ref[...])

    @pl.when(col_block < PANELS)
    def _():
        out_ref[...] = jnp.where(col_block == 0, p_left_ref[:, :NB], p_left_ref[:, NB:])

    @pl.when((col_block >= PANELS) & (row_block < PANELS))
    def _():
        out_ref[...] = jnp.zeros(out_ref.shape, bf16)

    @pl.when((col_block >= PANELS) & (row_block >= PANELS))
    def _():
        left = left_operand(left_rows_ref[...], scale_ref[...])
        value = jnp.exp(nt(left, right_ref[...]))
        noise = jnp.where(row_block == col_block, noise_ref[...], 0.0)
        value = add_diagonal(value, noise) - nt(p_left_ref[...], p_right_ref[...])
        out_ref[...] = value.astype(bf16)


VMEM = pl.BlockSpec(memory_space=pltpu.VMEM)
SMEM = pl.BlockSpec(memory_space=pltpu.SMEM)
PARAMS = pltpu.CompilerParams(vmem_limit_bytes=56 * 1024 * 1024)


def body(features, noise, owner_slot, inv_length):
    nrows = lax.axis_size("row")
    ncols = lax.axis_size("col")
    here = features.shape[0]
    count = nrows * ncols
    r = lax.axis_index("row").astype(jnp.int32)
    c = lax.axis_index("col").astype(jnp.int32)
    scale = inv_length.reshape(1, F)

    arranged, extra = pl.pallas_call(
        pack_kernel,
        out_shape=(
            jax.ShapeDtypeStruct((here, F), bf16),
            jax.ShapeDtypeStruct((8, here), bf16),
        ),
        in_specs=[VMEM] * 4,
        out_specs=(VMEM, VMEM),
        name="pack",
    )(features, noise.reshape(here, 1), owner_slot.reshape(here, 1), owner_slot.reshape(1, here))

    lead_send = jnp.concatenate([arranged[:16], extra], axis=0)
    lead_send = jnp.broadcast_to(lead_send[None], (count, 24, F))
    lead = lax.all_to_all(lead_send, ("row", "col"), 0, 0, tiled=True)

    groups = arranged.reshape(nrows, 8, F)
    to_row = jnp.broadcast_to(groups[:, None], (nrows, ncols, 8, F))
    to_col = jnp.broadcast_to(groups.reshape(1, 2, ncols, 8, F), (nrows, 2, ncols, 8, F))
    bulk_send = jnp.concatenate([to_row, to_col[:, 0], to_col[:, 1]], axis=2)
    bulk_send = bulk_send.reshape(count, 24, F)
    bulk_send, lead = lax.optimization_barrier((bulk_send, lead))
    bulk = lax.all_to_all(bulk_send, ("row", "col"), 0, 0, tiled=True)

    lead_samples = lead.reshape(nrows, ncols, 24, F)[:, :4, :16].reshape(nrows, 4, 2, 8, F)
    lead_samples = lead_samples.transpose(2, 1, 0, 3, 4).reshape(8, here, F)
    place = jnp.stack([r, c, c + ncols])
    blocks = jnp.stack([r, r + nrows, c, c + ncols, c + 2 * ncols, c + 3 * ncols])

    right, lead_noise, w, p21, slots, noises = pl.pallas_call(
        factor_kernel,
        out_shape=(
            jax.ShapeDtypeStruct((PANELS * NB, 4 * F), bf16),
            jax.ShapeDtypeStruct((PANELS * NB, 1), f32),
            jax.ShapeDtypeStruct((PANELS, 3, NB, NB), bf16),
            jax.ShapeDtypeStruct((NB, NB), bf16),
            jax.ShapeDtypeStruct((3, 8, here), f32),
            jax.ShapeDtypeStruct((3, 8, here), f32),
        ),
        in_specs=[SMEM] + [VMEM] * 4,
        out_specs=(VMEM,) * 6,
        scratch_shapes=[pltpu.VMEM((3, NB, NB), f32), pltpu.VMEM((NB, NB), f32)],
        compiler_params=PARAMS,
        name="factor",
    )(place, lead_samples, lead[:, 16], lead[:, 17], scale)

    bulk_samples = bulk.reshape(nrows, ncols, 3, 8, F).transpose(2, 1, 0, 3, 4)
    bulk_samples = bulk_samples.reshape(3, ncols, here, F)

    def kind_of(i):
        return jnp.where(i < 2, 0, 1 + i % 2), jnp.where(i < 2, i, (i - 2) // 2)

    whole = lambda *shape: pl.BlockSpec(shape, lambda i, b: (0,) * len(shape))
    rows, row_noise, panels = pl.pallas_call(
        panel_kernel,
        grid_spec=pltpu.PrefetchScalarGridSpec(
            num_scalar_prefetch=1,
            grid=(6,),
            in_specs=[
                pl.BlockSpec((1, 4, here, F), lambda i, b: (*kind_of(i), 0, 0)),
                whole(3, 8, here),
                whole(3, 8, here),
                whole(1, F),
                whole(PANELS * NB, 4 * F),
                whole(PANELS * NB, 1),
                whole(PANELS, 3, NB, NB),
                whole(NB, NB),
            ],
            out_specs=[
                pl.BlockSpec((NB, F), lambda i, b: (i, 0)),
                pl.BlockSpec((NB, 1), lambda i, b: (i, 0)),
                pl.BlockSpec((NB, PANELS * NB), lambda i, b: (i, 0)),
            ],
        ),
        out_shape=(
            jax.ShapeDtypeStruct((6 * NB, F), bf16),
            jax.ShapeDtypeStruct((6 * NB, 1), f32),
            jax.ShapeDtypeStruct((6 * NB, PANELS * NB), bf16),
        ),
        compiler_params=PARAMS,
        name="panel_rows",
    )(blocks, bulk_samples, slots, noises, scale, right, lead_noise, w, p21)

    return pl.pallas_call(
        tile_kernel,
        grid_spec=pltpu.PrefetchScalarGridSpec(
            num_scalar_prefetch=1,
            grid=(4, 2),
            in_specs=[
                pl.BlockSpec((NB, F), lambda j, i, b: (i, 0)),
                pl.BlockSpec((NB, F), lambda j, i, b: (2 + j, 0)),
                pl.BlockSpec((NB, 1), lambda j, i, b: (i, 0)),
                pl.BlockSpec((1, F), lambda j, i, b: (0, 0)),
                pl.BlockSpec((NB, PANELS * NB), lambda j, i, b: (i, 0)),
                pl.BlockSpec((NB, PANELS * NB), lambda j, i, b: (2 + j, 0)),
            ],
            out_specs=pl.BlockSpec((NB, NB), lambda j, i, b: (i, j)),
            scratch_shapes=[pltpu.VMEM((NB, 4 * F), bf16)],
        ),
        out_shape=jax.ShapeDtypeStruct((2 * NB, 4 * NB), bf16),
        compiler_params=PARAMS,
        name="tiles",
    )(blocks, rows, rows, row_noise, scale, panels, panels)


def solution(mesh):
    in_specs = (P(("row", "col"), None), P(("row", "col")), P(("row", "col")), P())
    out_specs = P("row", "col")
    return jax.shard_map(body, mesh=mesh, in_specs=in_specs, out_specs=out_specs, check_vma=False)
```

```python
import jax
import jax.numpy as jnp
from jax import lax
from jax.experimental import pallas as pl
from jax.experimental.pallas import tpu as pltpu
from jax.sharding import PartitionSpec as P

NB = 512
PANELS = 2
F = 128
f32 = jnp.float32
bf16 = jnp.bfloat16


def split3(x):
    h = x.astype(bf16)
    r = x - h.astype(f32)
    m = r.astype(bf16)
    return h, m, (r - m.astype(f32)).astype(bf16)


def split2(x):
    h = x.astype(bf16)
    return h, (x - h.astype(f32)).astype(bf16)


def left4(pieces):
    h, m = pieces
    return jnp.concatenate([h, h, m, m], axis=1)


def right4(pieces, axis):
    h, m = pieces
    return jnp.concatenate([h, m, h, m], axis=axis)


def left3(pieces):
    h, m = pieces
    return jnp.concatenate([h, h, m], axis=1)


def right3(pieces):
    h, m = pieces
    return jnp.concatenate([h, m, h], axis=1)


def nt(x, y):
    return lax.dot_general(x, y, (((1,), (1,)), ((), ())), preferred_element_type=f32)


def nn(x, y):
    return lax.dot_general(x, y, (((1,), (0,)), ((), ())), preferred_element_type=f32)


def iota(shape, dim):
    return lax.broadcasted_iota(jnp.int32, shape, dim)


def pack_kernel(feat_ref, noise_ref, slot_ref, sorted_ref, lead_ref):
    n = feat_ref.shape[0]
    eye = iota((n, n), 0) == iota((n, n), 1)
    row = slot_ref[...].astype(f32)
    col = jnp.sum(jnp.where(eye, row, 0.0), axis=1, keepdims=True)
    noise = noise_ref[...].astype(bf16).astype(f32)
    noise = jnp.sum(jnp.where(eye, noise, 0.0), axis=1, keepdims=True)
    local = (slot_ref[...] % n).astype(f32)
    local = jnp.sum(jnp.where(eye, local, 0.0), axis=1, keepdims=True)
    rank_col = jnp.sum((row < col).astype(f32), axis=1, keepdims=True)
    rank_row = jnp.sum((col < row).astype(f32), axis=0, keepdims=True)
    pick = (iota((n, n), 0).astype(f32) == rank_row).astype(bf16)
    arranged = nn(pick, feat_ref[...].astype(bf16))
    sorted_ref[...] = arranged.astype(bf16)
    back = rank_col == iota((n, n), 1).astype(f32)
    slots = jnp.sum(jnp.where(back, local, 0.0), axis=0, keepdims=True)
    noises = jnp.sum(jnp.where(back, noise, 0.0), axis=0, keepdims=True)
    which = iota((8, n), 0)
    extra = jnp.where(which == 0, slots, jnp.where(which == 1, noises, 0.0))
    block = jnp.concatenate([arranged[:16], extra], axis=0).astype(bf16)
    lead_ref[...] = jnp.broadcast_to(block[None], lead_ref.shape)


def spread_rows(table, target):
    n = table.shape[0]
    lane = iota((n, n), 1)
    mine = jnp.where(lane // 8 == target, table, jnp.zeros_like(table))
    comb = (iota((n, n), 0) % 8 == iota((n, n), 1) % 8).astype(bf16)
    spread = nn(mine, comb).reshape(n // 8, 8, n)
    take = iota((n // 8, 8, n), 2) // 8 == iota((n // 8, 8, n), 0)
    return jnp.sum(jnp.where(take, spread, 0.0), axis=0)


def place_range(slots, noises, samples):
    n = samples.shape[0]
    hot = iota((n, n), 0).astype(f32) == slots
    rows = nn(hot.astype(bf16), samples).astype(bf16)
    noise = jnp.sum(jnp.where(hot, noises, 0.0), axis=1, keepdims=True)
    return rows, noise


def fill_lanes(values, width):
    lane = iota((values[0].shape[0], width), 1)
    out = jnp.zeros((values[0].shape[0], width), f32)
    for i, v in enumerate(values):
        out = jnp.where(lane == i, v, out)
    return out.astype(bf16)


def half_norm(x, scale):
    return -0.5 * jnp.sum(x * x * scale, axis=1, keepdims=True)


def left_operand(rows, scale):
    h, m, l = split3(half_norm(rows.astype(f32), scale))
    extra = fill_lanes([1.0 + 0.0 * h.astype(f32)] * 3 + [h.astype(f32), m.astype(f32), l.astype(f32)], F)
    return jnp.concatenate([rows, rows, rows, extra], axis=1)


def right_operand(rows, scale):
    x = rows.astype(f32)
    h, m, l = split3(half_norm(x, scale))
    extra = fill_lanes([h.astype(f32), m.astype(f32), l.astype(f32)] + [1.0 + 0.0 * h.astype(f32)] * 3, F)
    return jnp.concatenate([*split3(x * scale), extra], axis=1)


def add_diagonal(value, noise):
    n = value.shape[0]
    return value + jnp.where(iota((n, n), 0) == iota((n, n), 1), noise, 0.0)


def lane(x, j):
    return jnp.broadcast_to(x[:, j : j + 1], (8, 128))


def invert_factor(block, spill_ref):
    def sub(q, k):
        return jnp.broadcast_to(spill_ref[q, k : k + 1, :], (8, 128))

    ri = iota((8, 128), 0)
    ci = iota((8, 128), 1)
    a = [block[8 * i : 8 * i + 8, :] for i in range(16)]
    b = [(ri + 8 * i == ci).astype(f32) for i in range(16)]
    out = []
    for g in range(16):
        o = 16 * (g % 2)
        cb = [lane(a[g], 8 * g + k) for k in range(8)]
        for k in range(8):
            spill_ref[o + k] = cb[k]
        spill_ref[o + 8] = a[g]
        spill_ref[o + 9] = b[g]
        d = [[sub(o + k, r) if r >= k else None for k in range(8)] for r in range(8)]
        ar = [sub(o + 8, k) for k in range(8)]
        br = [sub(o + 9, k) for k in range(8)]
        more = g + 1 < 16
        cc = [lane(a[g + 1], 8 * g + k) for k in range(8)] if more else None
        rs = [None] * 8
        l = [[None] * 8 for _ in range(8)]
        for k in range(8):
            rs[k] = lax.rsqrt(d[k][k])
            for m in range(k + 1, 8):
                l[m][k] = d[m][k] * rs[k]
            for m in range(k + 1, 8):
                for j in range(k + 1, m + 1):
                    d[m][j] = d[m][j] - l[m][k] * l[j][k]
            ar[k] = ar[k] * rs[k]
            br[k] = br[k] * rs[k]
            if more:
                cc[k] = cc[k] * rs[k]
            for m in range(k + 1, 8):
                ar[m] = ar[m] - l[m][k] * ar[k]
                br[m] = br[m] - l[m][k] * br[k]
                if more:
                    cc[m] = cc[m] - l[m][k] * cc[k]
            if more:
                a[g + 1] = a[g + 1] - cc[k] * ar[k]
                b[g + 1] = b[g + 1] - cc[k] * br[k]
        v = br[7]
        for k in range(7):
            v = jnp.where(ri == k, br[k], v)
        out.append(v)
        if g + 2 < 16:
            z = [None] * 8
            y = [None] * 8
            for k in range(7, -1, -1):
                zz = ar[k]
                yy = br[k]
                for m in range(7, k, -1):
                    zz = zz - l[m][k] * z[m]
                    yy = yy - l[m][k] * y[m]
                z[k] = zz * rs[k]
                y[k] = yy * rs[k]
            for i in range(g + 2, 16):
                ai = a[i]
                bi = b[i]
                for k in range(8):
                    c = lane(a[i], 8 * g + k)
                    ai = ai - c * z[k]
                    bi = bi - c * y[k]
                a[i] = ai
                b[i] = bi
    return jnp.concatenate(out, axis=0)


def invert_panel(a_ref, w_ref, spill_ref):
    w_ref[...] = jnp.zeros((NB, NB), f32)
    for s in range(0, NB, 128):
        e = s + 128
        w = invert_factor(a_ref[s:e, s:e], spill_ref)
        pieces = split2(w)
        wl = left4(pieces)
        if e < NB:
            low = nt(left4(split2(a_ref[e:NB, s:e])), right4(pieces, 1))
            low_pieces = split2(low)
            low_left = left4(low_pieces)
            a_ref[e:NB, e:NB] = a_ref[e:NB, e:NB] - nt(low_left, right4(low_pieces, 1))
        if s > 0:
            w_ref[s:e, 0:s] = nn(wl, right4(split2(w_ref[s:e, 0:s]), 0))
        w_ref[s:e, s:e] = w
        if e < NB:
            w_ref[e:NB, 0:e] = w_ref[e:NB, 0:e] - nn(low_left, right4(split2(w_ref[s:e, 0:e]), 0))


def times_inverse(left, pieces):
    half = NB // 2
    lp = split2(left)
    top = nt(left3([p[:, :half] for p in lp]), right3([p[:half, :half] for p in pieces]))
    bottom = nt(left3(lp), right3([p[half:, :] for p in pieces]))
    return jnp.concatenate([top, bottom], axis=1)


def factor_kernel(
    block_ref, samples_ref, slot_ref, noise_ref, scale_ref,
    right_ref, lead_noise_ref, w_ref, p21_ref, slots_ref, noises_ref, a_ref, inv_ref, spill_ref,
):
    scale = scale_ref[...]
    slot_table = slot_ref[...]
    noise_table = noise_ref[...]
    for panel in range(PANELS):
        slots = spread_rows(slot_table, panel)
        noises = spread_rows(noise_table, panel)
        rows = []
        for i in range(4):
            placed, noise = place_range(
                slots[i : i + 1, :], noises[i : i + 1, :], samples_ref[panel * 4 + i]
            )
            rows.append(placed)
            lead_noise_ref[panel * NB + i * 128 : panel * NB + (i + 1) * 128, :] = noise
        rows = jnp.concatenate(rows, axis=0)
        right_ref[panel * NB : (panel + 1) * NB, :] = right_operand(rows, scale)
        left = left_operand(rows, scale)
        for other in range(panel + 1):
            value = jnp.exp(nt(left, right_ref[other * NB : (other + 1) * NB, :]))
            if other == panel:
                value = add_diagonal(value, lead_noise_ref[panel * NB : (panel + 1) * NB, :])
            a_ref[panel + other] = value

    for kind in range(3):
        target = block_ref[(0, 2, 3)[kind]]
        slots_ref[kind] = spread_rows(slot_table, target)
        noises_ref[kind] = spread_rows(noise_table, target)

    def one_panel(panel, carry):
        invert_panel(a_ref.at[0], inv_ref, spill_ref)
        pieces = split2(inv_ref[...])
        for i in range(2):
            w_ref[panel, i] = pieces[i]

        @pl.when(panel == 0)
        def _():
            p21 = times_inverse(a_ref[1], pieces).astype(bf16)
            p21_ref[...] = p21
            a_ref[0] = a_ref[2] - nt(p21, p21)

        return carry

    lax.fori_loop(0, PANELS, one_panel, 0)


def kind_of(step):
    step = jnp.minimum(step, 5)
    return jnp.where(step < 2, 0, 1 + step % 2), jnp.where(step < 2, step, (step - 2) // 2)


def output_kernel(
    block_ref, samples_ref, slots_ref, noises_ref, scale_ref, lead_ref, lead_noise_ref,
    w_ref, p21_ref, out_ref, p_ref, left_ref, right_ref, noise_ref, k_ref,
):
    step = pl.program_id(0)

    @pl.when(step < 6)
    def _():
        kind, half = kind_of(step)
        block = block_ref[step]
        rows = []
        for i in range(4):
            placed, noise = place_range(
                slots_ref[kind, pl.ds(4 * half + i, 1), :],
                noises_ref[kind, pl.ds(4 * half + i, 1), :],
                samples_ref[:, i].reshape(128, F),
            )
            rows.append(placed)
            noise_ref[step, i * 128 : (i + 1) * 128, :] = noise
        rows = jnp.concatenate(rows, axis=0)
        scale = scale_ref[...]
        left = left_operand(rows, scale)

        @pl.when(step < 2)
        def _():
            left_ref[step] = left

        @pl.when(step >= 2)
        def _():
            right_ref[step - 2] = right_operand(rows, scale)

        for panel in range(PANELS):
            value = jnp.exp(nt(left, lead_ref[panel * NB : (panel + 1) * NB, :]))
            k_ref[panel] = value

        @pl.when(block < PANELS)
        def _():
            k_ref[block] = add_diagonal(k_ref[block], lead_noise_ref[pl.ds(block * NB, NB), :])

        p1 = times_inverse(k_ref[0], [w_ref[0, i] for i in range(2)]).astype(bf16)
        second = k_ref[1] - nt(p1, p21_ref[...])
        p2 = times_inverse(second, [w_ref[1, i] for i in range(2)]).astype(bf16)
        p_ref[step, :, :NB] = p1
        p_ref[step, :, NB:] = jnp.where(block >= 1, p2, jnp.zeros_like(p2))

    @pl.when(step >= 6)
    def _():
        i = (step - 6) % 2
        j = (step - 6) // 2
        row_block = block_ref[i]
        col_block = block_ref[2 + j]

        @pl.when(col_block == 0)
        def _():
            out_ref[...] = p_ref[i, :, :NB]

        @pl.when(col_block == 1)
        def _():
            out_ref[...] = p_ref[i, :, NB:]

        @pl.when((col_block >= PANELS) & (row_block < PANELS))
        def _():
            out_ref[...] = jnp.zeros(out_ref.shape, bf16)

        @pl.when((col_block >= PANELS) & (row_block >= PANELS))
        def _():
            value = jnp.exp(nt(left_ref[i], right_ref[j])) - nt(p_ref[i], p_ref[2 + j])

            @pl.when(row_block != col_block)
            def _():
                out_ref[...] = value.astype(bf16)

            @pl.when(row_block == col_block)
            def _():
                out_ref[...] = add_diagonal(value, noise_ref[i]).astype(bf16)


VMEM = pl.BlockSpec(memory_space=pltpu.VMEM)
SMEM = pl.BlockSpec(memory_space=pltpu.SMEM)
PARAMS = pltpu.CompilerParams(vmem_limit_bytes=56 * 1024 * 1024)


def body(features, noise, owner_slot, inv_length):
    nrows = lax.axis_size("row")
    ncols = lax.axis_size("col")
    here = features.shape[0]
    count = nrows * ncols
    r = lax.axis_index("row").astype(jnp.int32)
    c = lax.axis_index("col").astype(jnp.int32)
    scale = inv_length.reshape(1, F)

    arranged, lead_send = pl.pallas_call(
        pack_kernel,
        out_shape=(
            jax.ShapeDtypeStruct((here, F), bf16),
            jax.ShapeDtypeStruct((count, 24, F), bf16),
        ),
        in_specs=[VMEM] * 3,
        out_specs=(VMEM, VMEM),
        name="pack",
    )(features, noise.reshape(1, here), owner_slot.reshape(1, here))
    lead = lax.all_to_all(lead_send, ("row", "col"), 0, 0, tiled=True)

    groups = arranged.reshape(nrows, 8, F)
    to_row = jnp.broadcast_to(groups[:, None], (nrows, ncols, 8, F))
    to_col = jnp.broadcast_to(groups.reshape(1, 2, ncols, 8, F), (nrows, 2, ncols, 8, F))
    bulk_send = jnp.concatenate([to_row, to_col[:, 0], to_col[:, 1]], axis=2)
    bulk_send = bulk_send.reshape(count, 24, F)
    bulk_send, lead = lax.optimization_barrier((bulk_send, lead))
    bulk = lax.all_to_all(bulk_send, ("row", "col"), 0, 0, tiled=True)

    lead_samples = lead.reshape(nrows, ncols, 24, F)[:, :4, :16].reshape(nrows, 4, 2, 8, F)
    lead_samples = lead_samples.transpose(2, 1, 0, 3, 4).reshape(8, here, F)
    blocks = jnp.stack([r, r + nrows, c, c + ncols, c + 2 * ncols, c + 3 * ncols])

    right, lead_noise, w, p21, slots, noises = pl.pallas_call(
        factor_kernel,
        out_shape=(
            jax.ShapeDtypeStruct((PANELS * NB, 4 * F), bf16),
            jax.ShapeDtypeStruct((PANELS * NB, 1), f32),
            jax.ShapeDtypeStruct((PANELS, 2, NB, NB), bf16),
            jax.ShapeDtypeStruct((NB, NB), bf16),
            jax.ShapeDtypeStruct((3, 8, here), f32),
            jax.ShapeDtypeStruct((3, 8, here), f32),
        ),
        in_specs=[SMEM] + [VMEM] * 4,
        out_specs=(VMEM,) * 6,
        scratch_shapes=[
            pltpu.VMEM((3, NB, NB), f32),
            pltpu.VMEM((NB, NB), f32),
            pltpu.VMEM((32, 8, 128), f32),
        ],
        compiler_params=PARAMS,
        name="factor",
    )(blocks, lead_samples, lead[:, 16], lead[:, 17], scale)

    whole = lambda *shape: pl.BlockSpec(shape, lambda i, b: (0,) * len(shape))

    def samples_of(i, b):
        kind, half = kind_of(i)
        return 0, half, kind, 0

    def tile_of(i, b):
        tile = jnp.maximum(i - 6, 0)
        return tile % 2, tile // 2

    return pl.pallas_call(
        output_kernel,
        grid_spec=pltpu.PrefetchScalarGridSpec(
            num_scalar_prefetch=1,
            grid=(14,),
            in_specs=[
                pl.BlockSpec((nrows, 4, 8, F), samples_of),
                whole(3, 8, here),
                whole(3, 8, here),
                whole(1, F),
                whole(PANELS * NB, 4 * F),
                whole(PANELS * NB, 1),
                whole(PANELS, 2, NB, NB),
                whole(NB, NB),
            ],
            out_specs=pl.BlockSpec((NB, NB), tile_of),
            scratch_shapes=[
                pltpu.VMEM((6, NB, PANELS * NB), bf16),
                pltpu.VMEM((2, NB, 4 * F), bf16),
                pltpu.VMEM((4, NB, 4 * F), bf16),
                pltpu.VMEM((6, NB, 1), f32),
                pltpu.VMEM((PANELS, NB, NB), f32),
            ],
        ),
        out_shape=jax.ShapeDtypeStruct((2 * NB, 4 * NB), bf16),
        compiler_params=PARAMS,
        name="output",
    )(
        blocks, bulk.reshape(nrows, ncols, 24, F), slots, noises, scale, right, lead_noise, w, p21
    )


def solution(mesh):
    in_specs = (P(("row", "col"), None), P(("row", "col")), P(("row", "col")), P())
    out_specs = P("row", "col")
    return jax.shard_map(body, mesh=mesh, in_specs=in_specs, out_specs=out_specs, check_vma=False)
```

```python
import jax
import jax.numpy as jnp
from jax import lax
from jax.experimental import pallas as pl
from jax.experimental.pallas import tpu as pltpu
from jax.sharding import PartitionSpec as P

NB = 512
PANELS = 2
F = 128
f32 = jnp.float32
bf16 = jnp.bfloat16


def split2(x):
    h = x.astype(bf16)
    return h, (x - h.astype(f32)).astype(bf16)


def left4(pieces):
    h, m = pieces
    return jnp.concatenate([h, h, m, m], axis=1)


def right4(pieces, axis):
    h, m = pieces
    return jnp.concatenate([h, m, h, m], axis=axis)


def left3(pieces):
    h, m = pieces
    return jnp.concatenate([h, h, m], axis=1)


def right3(pieces):
    h, m = pieces
    return jnp.concatenate([h, m, h], axis=1)


def nt(x, y):
    return lax.dot_general(x, y, (((1,), (1,)), ((), ())), preferred_element_type=f32)


def nn(x, y):
    return lax.dot_general(x, y, (((1,), (0,)), ((), ())), preferred_element_type=f32)


def iota(shape, dim):
    return lax.broadcasted_iota(jnp.int32, shape, dim)


def pack_kernel(feat_ref, noise_ref, slot_ref, sorted_ref, lead_ref):
    n = feat_ref.shape[0]
    eye = iota((n, n), 0) == iota((n, n), 1)
    row = slot_ref[...].astype(f32)
    col = jnp.sum(jnp.where(eye, row, 0.0), axis=1, keepdims=True)
    noise = noise_ref[...].astype(bf16).astype(f32)
    noise = jnp.sum(jnp.where(eye, noise, 0.0), axis=1, keepdims=True)
    local = (slot_ref[...] % n).astype(f32)
    local = jnp.sum(jnp.where(eye, local, 0.0), axis=1, keepdims=True)
    rank_col = jnp.sum((row < col).astype(f32), axis=1, keepdims=True)
    rank_row = jnp.sum((col < row).astype(f32), axis=0, keepdims=True)
    arranged = nn((iota((n, n), 0).astype(f32) == rank_row).astype(bf16), feat_ref[...].astype(bf16))
    sorted_ref[...] = arranged.astype(bf16)
    back = rank_col == iota((n, n), 1).astype(f32)
    slots = jnp.sum(jnp.where(back, local, 0.0), axis=0, keepdims=True)
    noises = jnp.sum(jnp.where(back, noise, 0.0), axis=0, keepdims=True)
    c = lax.axis_index("col").astype(jnp.int32)
    which = iota((8, n), 0)
    extra = jnp.where(which == c, slots, jnp.where((which + 4) % 8 == c, noises, 0.0))
    block = jnp.concatenate([arranged[:16], extra], axis=0).astype(bf16)
    lead_ref[...] = jnp.broadcast_to(block[None], lead_ref.shape)


def spread_rows(table, target):
    n = table.shape[0]
    lane = iota((n, n), 1)
    mine = jnp.where(lane // 8 == target, table, jnp.zeros_like(table))
    comb = (iota((n, n), 0) % 8 == iota((n, n), 1) % 8).astype(bf16)
    spread = nn(mine, comb).reshape(n // 8, 8, n)
    take = iota((n // 8, 8, n), 2) // 8 == iota((n // 8, 8, n), 0)
    return jnp.sum(jnp.where(take, spread, 0.0), axis=0)


def read_tables(lead_ref):
    nrows = lead_ref.shape[0]
    slots, noises = [], []
    low = iota((8, 128), 0) < 4
    for r in range(nrows):
        parts = [lead_ref[r, c, 16:24, :].astype(f32) for c in range(8)]
        first = (parts[0] + parts[1]) + (parts[2] + parts[3])
        last = (parts[4] + parts[5]) + (parts[6] + parts[7])
        slots.append(jnp.where(low, first, last))
        other = jnp.where(low, last, first)
        noises.append(jnp.concatenate([other[4:], other[:4]], axis=0))
    return (
        jnp.concatenate(slots, axis=0).astype(bf16),
        jnp.concatenate(noises, axis=0).astype(bf16),
    )


def positions():
    nrows = lax.axis_size("row")
    ncols = lax.axis_size("col")
    r = lax.axis_index("row").astype(jnp.int32)
    c = lax.axis_index("col").astype(jnp.int32)
    return [r, r + nrows, c, c + 2 * ncols, c + ncols, c + 3 * ncols]


def pick(values, index):
    out = values[0]
    for i, v in enumerate(values[1:]):
        out = jnp.where(index == i + 1, v, out)
    return out


def one_hot(slots):
    n = slots.shape[1]
    return (iota((n, n), 0).astype(f32) == slots).astype(bf16)


def place_noise(hot, noises):
    return nt(hot, jnp.broadcast_to(noises.astype(bf16), hot.shape))


def norm_pieces(rows, scale):
    x = rows.astype(f32)
    return jnp.concatenate(split2(-0.5 * (x * x * scale)), axis=1)


def left_operand(rows, scale):
    norm = nn(norm_pieces(rows, scale), jnp.ones((2 * F, 128), bf16))
    return jnp.concatenate([rows, rows], axis=1), norm


def right_operand(rows, scale):
    norm = nt(jnp.ones((8, 2 * F), bf16), norm_pieces(rows, scale))
    return jnp.concatenate(split2(rows.astype(f32) * scale), axis=1), norm


def kernel_values(left, left_norm, right, right_norm):
    wide = jnp.concatenate([left_norm] * (right.shape[0] // 128), axis=1)
    return jnp.exp(nt(left, right) + wide + right_norm[0:1, :])


def add_diagonal(value, noise, start=0):
    n, width = value.shape
    eye = iota((128, 128), 0) == iota((128, 128), 1)
    bands = []
    for i in range(0, n, 128):
        band = value[i : i + 128, :]
        at = start + i
        square = band[:, at : at + 128] + jnp.where(eye, noise[i : i + 128, :], 0.0)
        parts = [band[:, :at], square, band[:, at + 128 :]]
        bands.append(jnp.concatenate([p for p in parts if p.shape[1]], axis=1))
    return jnp.concatenate(bands, axis=0)


def lane(x, j):
    return jnp.broadcast_to(x[:, j : j + 1], (8, 128))


def invert_factor(block, spill_ref, filler=None):
    def sub(q, k):
        return jnp.broadcast_to(spill_ref[q, k : k + 1, :], (8, 128))

    ri = iota((8, 128), 0)
    ci = iota((8, 128), 1)
    a = [block[8 * i : 8 * i + 8, :] for i in range(16)]
    b = [(ri + 8 * i == ci).astype(f32) for i in range(16)]
    out = []
    held = None
    for g in range(16):
        even = g % 2 == 0
        o = 32 * (g % 2)
        cb = [lane(a[g], 8 * g + k) for k in range(8)] if even else held
        cc = [lane(a[g + 1], 8 * g + k) for k in range(8)] if even else None
        nb = [lane(a[g + 1], 8 * g + 8 + k) for k in range(8)] if even else None
        for k in range(8):
            spill_ref[o + k] = cb[k]
        spill_ref[o + 8] = a[g]
        spill_ref[o + 9] = b[g]
        d = [[sub(o + k, r) if r >= k else None for k in range(8)] for r in range(8)]
        ar = [sub(o + 8, k) for k in range(8)]
        br = [sub(o + 9, k) for k in range(8)]
        rs = [None] * 8
        l = [[None] * 8 for _ in range(8)]

        def apply(k):
            ar[k] = ar[k] * rs[k]
            br[k] = br[k] * rs[k]
            if even:
                cc[k] = cc[k] * rs[k]
            for m in range(k + 1, 8):
                ar[m] = ar[m] - l[m][k] * ar[k]
                br[m] = br[m] - l[m][k] * br[k]
                if even:
                    cc[m] = cc[m] - l[m][k] * cc[k]
            if even:
                a[g + 1] = a[g + 1] - cc[k] * ar[k]
                b[g + 1] = b[g + 1] - cc[k] * br[k]
                spill_ref[o + 16 + k] = cc[k]
                for q in range(8):
                    nb[q] = nb[q] - cc[k] * sub(o + 16 + k, q)

        for k in range(0, 8, 2):
            r0 = lax.rsqrt(d[k][k])
            det = d[k][k] * d[k + 1][k + 1] - d[k + 1][k] * d[k + 1][k]
            rs[k] = r0
            rs[k + 1] = lax.rsqrt(det) * (d[k][k] * r0)
            for m in range(k + 1, 8):
                l[m][k] = d[m][k] * r0
            for m in range(k + 2, 8):
                l[m][k + 1] = (d[m][k + 1] - l[m][k] * l[k + 1][k]) * rs[k + 1]
            for m in range(k + 2, 8):
                for j in range(k + 2, m + 1):
                    d[m][j] = (d[m][j] - l[m][k] * l[j][k]) - l[m][k + 1] * l[j][k + 1]
            apply(k)
            apply(k + 1)
        if even:
            held = nb
        v = br[7]
        for k in range(7):
            v = jnp.where(ri == k, br[k], v)
        out.append(v)
        if filler is not None:
            next(filler, None)
        first = g + 2 if even else g + 1
        if first < 16:
            z = [None] * 8
            y = [None] * 8
            for k in range(7, -1, -1):
                zz = ar[k]
                yy = br[k]
                for m in range(7, k, -1):
                    zz = zz - l[m][k] * z[m]
                    yy = yy - l[m][k] * y[m]
                z[k] = zz * rs[k]
                y[k] = yy * rs[k]
            for i in range(first, 16):
                ai = a[i]
                bi = b[i]
                for k in range(8):
                    c = lane(a[i], 8 * g + k)
                    ai = ai - c * z[k]
                    bi = bi - c * y[k]
                a[i] = ai
                b[i] = bi
    return jnp.concatenate(out, axis=0)


def invert_panel(a_ref, w_ref, spill_ref, fillers=(None,) * 4):
    w_ref[...] = jnp.zeros((NB, NB), f32)
    for s in range(0, NB, 128):
        e = s + 128
        filler = fillers[s // 128]
        w = invert_factor(a_ref[s:e, s:e], spill_ref, filler)
        if filler is not None:
            for _ in filler:
                pass
        pieces = split2(w)
        wl = left4(pieces)
        if e < NB:
            low = nt(left4(split2(a_ref[e:NB, s:e])), right4(pieces, 1))
            low_pieces = split2(low)
            low_left = left4(low_pieces)
            a_ref[e:NB, e:NB] = a_ref[e:NB, e:NB] - nt(low_left, right4(low_pieces, 1))
        if s > 0:
            w_ref[s:e, 0:s] = nn(wl, right4(split2(w_ref[s:e, 0:s]), 0))
        w_ref[s:e, s:e] = w
        if e < NB:
            w_ref[e:NB, 0:e] = w_ref[e:NB, 0:e] - nn(low_left, right4(split2(w_ref[s:e, 0:e]), 0))


def times_inverse(left, pieces):
    half = NB // 2
    lp = split2(left)
    top = nt(left3([p[:, :half] for p in lp]), right3([p[:half, :half] for p in pieces]))
    bottom = nt(left3(lp), right3([p[half:, :] for p in pieces]))
    return jnp.concatenate([top, bottom], axis=1)


def factor_kernel(
    lead_ref, scale_ref,
    right_ref, norm_ref, lead_noise_ref, w_ref, p21_ref, slots_ref, noises_ref, next_ref,
    a_ref, inv_ref, spill_ref,
):
    scale = scale_ref[...]
    slot_table, noise_table = read_tables(lead_ref)

    def lead_rows(panel):
        slots = spread_rows(slot_table, panel)
        noises = spread_rows(noise_table, panel)
        rows = []
        for c in range(4):
            hot = one_hot(slots[c : c + 1, :])
            at = panel * NB + c * 128
            rows.append(nn(hot, lead_ref[:, c, 8 * panel : 8 * panel + 8, :].reshape(128, F)))
            lead_noise_ref[at : at + 128, :] = place_noise(hot, noises[c : c + 1, :])
        rows = jnp.concatenate(rows, axis=0).astype(bf16)
        right_ref[panel], norm_ref[panel] = right_operand(rows, scale)
        return left_operand(rows, scale)

    a_ref[0] = add_diagonal(
        kernel_values(*lead_rows(0), right_ref[0], norm_ref[0]), lead_noise_ref[:NB, :]
    )

    def rest():
        left = lead_rows(1)
        yield
        a_ref[1] = kernel_values(*left, right_ref[0], norm_ref[0])
        yield
        a_ref[2] = add_diagonal(
            kernel_values(*left, right_ref[1], norm_ref[1]), lead_noise_ref[NB:, :]
        )
        yield
        blocks = positions()
        for kind in range(3):
            slots_ref[kind] = spread_rows(slot_table, blocks[2 * kind])
            noises_ref[kind] = spread_rows(noise_table, blocks[2 * kind])
            yield

    invert_panel(a_ref.at[0], inv_ref, spill_ref, (rest(), None, None, None))
    pieces = split2(inv_ref[...])
    for i in range(2):
        w_ref[i] = pieces[i]
    p21 = times_inverse(a_ref[1], pieces).astype(bf16)
    p21_ref[...] = p21
    next_ref[...] = a_ref[2] - nt(p21, p21)


UNIT = 256


def second_kernel(
    bulk_ref, slots_ref, noises_ref, scale_ref, right_ref, norm_ref, lead_noise_ref,
    w_ref, next_ref, rows_ref, row_noise_ref, p1_ref, w2_ref, a_ref, inv_ref, spill_ref,
):
    a_ref[...] = next_ref[...]
    scale = scale_ref[...]
    half = NB // 2
    blocks = positions()

    def unit(index):
        block = blocks[index // 2]
        at = slice(index * UNIT, (index + 1) * UNIT)
        rows = []
        for i in range(2):
            kind, c = divmod(index * 2 + i, 8)
            hot = one_hot(slots_ref[kind, c : c + 1, :])
            rows.append(nn(hot, bulk_ref[:, c, 8 * kind : 8 * kind + 8, :].reshape(128, F)))
            if kind == 0:
                row_noise_ref[c * 128 : c * 128 + 128, :] = place_noise(
                    hot, noises_ref[kind, c : c + 1, :]
                )
        rows = jnp.concatenate(rows, axis=0).astype(bf16)
        rows_ref[at, :] = rows
        yield
        value = kernel_values(*left_operand(rows, scale), right_ref[0], norm_ref[0])
        lo = index % 2 * UNIT
        lead = jnp.where(block == 0, lead_noise_ref[lo : lo + UNIT, :], 0.0)
        pieces = split2(add_diagonal(value, lead, lo))
        yield
        top = nt(
            left3([p[:, :half] for p in pieces]),
            right3([w_ref[i, :half, :half] for i in range(2)]),
        )
        p1_ref[at, :half] = top.astype(bf16)
        yield
        bottom = nt(left3(pieces), right3([w_ref[i, half:, :] for i in range(2)]))
        p1_ref[at, half:] = bottom.astype(bf16)
        yield

    def units(first, last):
        for index in range(first, last):
            yield from unit(index)

    invert_panel(a_ref, inv_ref, spill_ref, [units(3 * i, 3 * i + 3) for i in range(4)])
    pieces = split2(inv_ref[...])
    for i in range(2):
        w2_ref[i] = pieces[i]


def output_kernel(
    rows_ref, row_noise_ref, scale_ref, lead_ref, lead_norm_ref, lead_noise_ref,
    p1_ref, p21_ref, w_ref, out_ref, p_ref, left_ref, left_norm_ref, right_ref, right_norm_ref,
):
    step = pl.program_id(0)
    blocks = positions()
    tall = 2 * NB

    @pl.when(step < 3)
    def _():
        pair = [pick(blocks[i::2], step) for i in range(2)]
        rows = rows_ref[...]
        scale = scale_ref[...]
        left, left_norm = left_operand(rows, scale)

        @pl.when(step == 0)
        def _():
            left_ref[...] = left
            left_norm_ref[...] = left_norm

        @pl.when(step >= 1)
        def _():
            right, norm = right_operand(rows, scale)
            for i in range(2):
                right_ref[2 * step - 2 + i] = right[i * NB : (i + 1) * NB, :]
                right_norm_ref[2 * step - 2 + i] = norm[:, i * NB : (i + 1) * NB]

        value = kernel_values(left, left_norm, lead_ref[1], lead_norm_ref[1])
        noise = lead_noise_ref[NB:, :]
        value = jnp.concatenate(
            [
                add_diagonal(value[i * NB : (i + 1) * NB, :], jnp.where(pair[i] == 1, noise, 0.0))
                for i in range(2)
            ],
            axis=0,
        )
        p1 = p1_ref[...]
        second = value - nt(p1, p21_ref[...])
        p2 = times_inverse(second, [w_ref[i] for i in range(2)])
        at = pl.multiple_of(step * tall, tall)
        p_ref[pl.ds(at, tall), :NB] = p1
        for i in range(2):
            kept = jnp.where(pair[i] >= 1, p2[i * NB : (i + 1) * NB, :], 0.0)
            p_ref[pl.ds(at + i * NB, NB), NB:] = kept.astype(bf16)

    @pl.when(step >= 3)
    def _():
        column = step - 3
        j = 2 * (column % 2) + column // 2
        col_block = pick(blocks[2:], j)

        @pl.when(col_block == 0)
        def _():
            out_ref[...] = p_ref[:tall, :NB]

        @pl.when(col_block == 1)
        def _():
            out_ref[...] = p_ref[:tall, NB:]

        @pl.when(col_block >= PANELS)
        def _():
            value = kernel_values(left_ref[...], left_norm_ref[...], right_ref[j], right_norm_ref[j])
            at = pl.multiple_of((2 + j) * NB, NB)
            value = value - nt(p_ref[:tall, :], p_ref[pl.ds(at, NB), :])
            for i in range(2):
                noise = row_noise_ref[i * NB : (i + 1) * NB, :]
                noise = jnp.where(blocks[i] == col_block, noise, 0.0)
                half = add_diagonal(value[i * NB : (i + 1) * NB, :], noise)
                half = jnp.where(blocks[i] >= PANELS, half, 0.0)
                out_ref[i * NB : (i + 1) * NB, :] = half.astype(bf16)


VMEM = pl.BlockSpec(memory_space=pltpu.VMEM)
SMEM = pl.BlockSpec(memory_space=pltpu.SMEM)
PARAMS = pltpu.CompilerParams(vmem_limit_bytes=56 * 1024 * 1024)


def body(features, noise, owner_slot, inv_length):
    nrows = lax.axis_size("row")
    ncols = lax.axis_size("col")
    here = features.shape[0]
    count = nrows * ncols
    scale = inv_length.reshape(1, F)

    arranged, lead_send = pl.pallas_call(
        pack_kernel,
        out_shape=(
            jax.ShapeDtypeStruct((here, F), bf16),
            jax.ShapeDtypeStruct((count, 24, F), bf16),
        ),
        in_specs=[VMEM] * 3,
        out_specs=(VMEM, VMEM),
        name="pack",
    )(features, noise.reshape(1, here), owner_slot.reshape(1, here))
    lead = lax.all_to_all(lead_send, ("row", "col"), 0, 0, tiled=True)

    groups = arranged.reshape(nrows, 8, F)
    to_row = jnp.broadcast_to(groups[:, None], (nrows, ncols, 8, F))
    to_col = jnp.broadcast_to(groups.reshape(1, 2, ncols, 8, F), (nrows, 2, ncols, 8, F))
    bulk_send = jnp.concatenate([to_row, to_col[:, 0], to_col[:, 1]], axis=2)
    bulk_send = bulk_send.reshape(count, 24, F)
    bulk_send, lead = lax.optimization_barrier((bulk_send, lead))
    bulk = lax.all_to_all(bulk_send, ("row", "col"), 0, 0, tiled=True)

    right, norm, lead_noise, w1, p21, slots, noises, trailing = pl.pallas_call(
        factor_kernel,
        out_shape=(
            jax.ShapeDtypeStruct((PANELS, NB, 2 * F), bf16),
            jax.ShapeDtypeStruct((PANELS, 8, NB), f32),
            jax.ShapeDtypeStruct((PANELS * NB, 128), f32),
            jax.ShapeDtypeStruct((2, NB, NB), bf16),
            jax.ShapeDtypeStruct((NB, NB), bf16),
            jax.ShapeDtypeStruct((3, 8, here), f32),
            jax.ShapeDtypeStruct((3, 8, here), f32),
            jax.ShapeDtypeStruct((NB, NB), f32),
        ),
        in_specs=[VMEM] * 2,
        out_specs=(VMEM,) * 8,
        scratch_shapes=[
            pltpu.VMEM((3, NB, NB), f32),
            pltpu.VMEM((NB, NB), f32),
            pltpu.VMEM((64, 8, 128), f32),
        ],
        compiler_params=PARAMS,
        name="first_panel",
    )(lead.reshape(nrows, ncols, 24, F), scale)

    rows, row_noise, p1, w2 = pl.pallas_call(
        second_kernel,
        out_shape=(
            jax.ShapeDtypeStruct((6 * NB, F), bf16),
            jax.ShapeDtypeStruct((2 * NB, 128), f32),
            jax.ShapeDtypeStruct((6 * NB, NB), bf16),
            jax.ShapeDtypeStruct((2, NB, NB), bf16),
        ),
        in_specs=[VMEM] * 9,
        out_specs=(VMEM,) * 4,
        scratch_shapes=[
            pltpu.VMEM((NB, NB), f32),
            pltpu.VMEM((NB, NB), f32),
            pltpu.VMEM((64, 8, 128), f32),
        ],
        compiler_params=PARAMS,
        name="second_panel",
    )(
        bulk.reshape(nrows, ncols, 24, F), slots, noises, scale, right, norm, lead_noise, w1,
        trailing,
    )

    whole = lambda *shape: pl.BlockSpec(shape, lambda i: (0,) * len(shape))
    tall = lambda *shape: pl.BlockSpec(shape, lambda i: (jnp.minimum(i, 2), 0))
    return pl.pallas_call(
        output_kernel,
        grid=(7,),
        in_specs=[
            tall(2 * NB, F),
            whole(2 * NB, 128),
            whole(1, F),
            whole(PANELS, NB, 2 * F),
            whole(PANELS, 8, NB),
            whole(PANELS * NB, 128),
            tall(2 * NB, NB),
            whole(NB, NB),
            whole(2, NB, NB),
        ],
        out_specs=pl.BlockSpec((2 * NB, NB), lambda i: (0, jnp.maximum(i - 3, 0))),
        scratch_shapes=[
            pltpu.VMEM((6 * NB, PANELS * NB), bf16),
            pltpu.VMEM((2 * NB, 2 * F), bf16),
            pltpu.VMEM((2 * NB, 128), f32),
            pltpu.VMEM((4, NB, 2 * F), bf16),
            pltpu.VMEM((4, 8, NB), f32),
        ],
        out_shape=jax.ShapeDtypeStruct((2 * NB, 4 * NB), bf16),
        compiler_params=PARAMS,
        name="output",
    )(rows, row_noise, scale, right, norm, lead_noise, p1, p21, w2)


def solution(mesh):
    in_specs = (P(("row", "col"), None), P(("row", "col")), P(("row", "col")), P())
    out_specs = P("row", "col")
    return jax.shard_map(body, mesh=mesh, in_specs=in_specs, out_specs=out_specs, check_vma=False)
```

```python
import itertools

import jax
import jax.numpy as jnp
from jax import lax
from jax.experimental import pallas as pl
from jax.experimental.pallas import tpu as pltpu
from jax.sharding import PartitionSpec as P

NB = 512
PANELS = 2
F = 128
f32 = jnp.float32
bf16 = jnp.bfloat16


def split2(x):
    h = x.astype(bf16)
    return h, (x - h.astype(f32)).astype(bf16)


def left4(pieces):
    h, m = pieces
    return jnp.concatenate([h, h, m, m], axis=1)


def right4(pieces, axis):
    h, m = pieces
    return jnp.concatenate([h, m, h, m], axis=axis)


def left3(pieces):
    h, m = pieces
    return jnp.concatenate([h, h, m], axis=1)


def right3(pieces):
    h, m = pieces
    return jnp.concatenate([h, m, h], axis=1)


def nt(x, y):
    return lax.dot_general(x, y, (((1,), (1,)), ((), ())), preferred_element_type=f32)


def nn(x, y):
    return lax.dot_general(x, y, (((1,), (0,)), ((), ())), preferred_element_type=f32)


def iota(shape, dim):
    return lax.broadcasted_iota(jnp.int32, shape, dim)


def pack_kernel(feat_ref, noise_ref, slot_ref, sorted_ref, lead_ref):
    n = feat_ref.shape[0]
    eye = iota((n, n), 0) == iota((n, n), 1)
    row = slot_ref[...].astype(f32)
    col = jnp.sum(jnp.where(eye, row, 0.0), axis=1, keepdims=True)
    noise = noise_ref[...].astype(bf16).astype(f32)
    noise = jnp.sum(jnp.where(eye, noise, 0.0), axis=1, keepdims=True)
    local = (slot_ref[...] % n).astype(f32)
    local = jnp.sum(jnp.where(eye, local, 0.0), axis=1, keepdims=True)
    rank_col = jnp.sum((row < col).astype(f32), axis=1, keepdims=True)
    rank_row = jnp.sum((col < row).astype(f32), axis=0, keepdims=True)
    arranged = nn((iota((n, n), 0).astype(f32) == rank_row).astype(bf16), feat_ref[...].astype(bf16))
    sorted_ref[...] = arranged.astype(bf16)
    back = rank_col == iota((n, n), 1).astype(f32)
    slots = jnp.sum(jnp.where(back, local, 0.0), axis=0, keepdims=True)
    noises = jnp.sum(jnp.where(back, noise, 0.0), axis=0, keepdims=True)
    c = lax.axis_index("col").astype(jnp.int32)
    which = iota((8, n), 0)
    extra = jnp.where(which == c, slots, jnp.where((which + 4) % 8 == c, noises, 0.0))
    block = jnp.concatenate([arranged[:16], extra], axis=0).astype(bf16)
    lead_ref[...] = jnp.broadcast_to(block[None], lead_ref.shape)


def spread_rows(table, target):
    n = table.shape[0]
    lane = iota((n, n), 1)
    mine = jnp.where(lane // 8 == target, table, jnp.zeros_like(table))
    comb = (iota((n, n), 0) % 8 == iota((n, n), 1) % 8).astype(bf16)
    spread = nn(mine, comb).reshape(n // 8, 8, n)
    take = iota((n // 8, 8, n), 2) // 8 == iota((n // 8, 8, n), 0)
    return jnp.sum(jnp.where(take, spread, 0.0), axis=0)


def read_tables(lead_ref):
    nrows = lead_ref.shape[0]
    slots, noises = [], []
    low = iota((8, 128), 0) < 4
    for r in range(nrows):
        parts = [lead_ref[r, c, 16:24, :].astype(f32) for c in range(8)]
        first = (parts[0] + parts[1]) + (parts[2] + parts[3])
        last = (parts[4] + parts[5]) + (parts[6] + parts[7])
        slots.append(jnp.where(low, first, last))
        other = jnp.where(low, last, first)
        noises.append(jnp.concatenate([other[4:], other[:4]], axis=0))
    return (
        jnp.concatenate(slots, axis=0).astype(bf16),
        jnp.concatenate(noises, axis=0).astype(bf16),
    )


def positions():
    nrows = lax.axis_size("row")
    ncols = lax.axis_size("col")
    r = lax.axis_index("row").astype(jnp.int32)
    c = lax.axis_index("col").astype(jnp.int32)
    return [r, r + nrows, c, c + 2 * ncols, c + ncols, c + 3 * ncols]


def pick(values, index):
    out = values[0]
    for i, v in enumerate(values[1:]):
        out = jnp.where(index == i + 1, v, out)
    return out


def one_hot(slots):
    n = slots.shape[1]
    return (iota((n, n), 0).astype(f32) == slots).astype(bf16)


def place_noise(hot, noises):
    return nt(hot, jnp.broadcast_to(noises.astype(bf16), hot.shape))


def norm_pieces(rows, scale):
    x = rows.astype(f32)
    return jnp.concatenate(split2(-0.5 * (x * x * scale)), axis=1)


def left_operand(rows, scale):
    norm = nn(norm_pieces(rows, scale), jnp.ones((2 * F, 128), bf16))
    return jnp.concatenate([rows, rows], axis=1), norm


def right_operand(rows, scale):
    norm = nt(jnp.ones((8, 2 * F), bf16), norm_pieces(rows, scale))
    return jnp.concatenate(split2(rows.astype(f32) * scale), axis=1), norm


def kernel_values(left, left_norm, right, right_norm):
    wide = jnp.concatenate([left_norm] * (right.shape[0] // 128), axis=1)
    return jnp.exp(nt(left, right) + wide + right_norm[0:1, :])


def add_diagonal(value, noise, start=0):
    n, width = value.shape
    eye = iota((128, 128), 0) == iota((128, 128), 1)
    bands = []
    for i in range(0, n, 128):
        band = value[i : i + 128, :]
        at = start + i
        square = band[:, at : at + 128] + jnp.where(eye, noise[i : i + 128, :], 0.0)
        parts = [band[:, :at], square, band[:, at + 128 :]]
        bands.append(jnp.concatenate([p for p in parts if p.shape[1]], axis=1))
    return jnp.concatenate(bands, axis=0)


def lane(x, j):
    return jnp.broadcast_to(x[:, j : j + 1], (8, 128))


def invert_factor(block, spill_ref, filler=None):
    def sub(q, k):
        return jnp.broadcast_to(spill_ref[q, k : k + 1, :], (8, 128))

    ri = iota((8, 128), 0)
    ci = iota((8, 128), 1)
    a = [block[8 * i : 8 * i + 8, :] for i in range(16)]
    b = [(ri + 8 * i == ci).astype(f32) for i in range(16)]
    out = []
    held = None
    for g in range(16):
        even = g % 2 == 0
        o = 32 * (g % 2)
        cb = [lane(a[g], 8 * g + k) for k in range(8)] if even else held
        cc = [lane(a[g + 1], 8 * g + k) for k in range(8)] if even else None
        nb = [lane(a[g + 1], 8 * g + 8 + k) for k in range(8)] if even else None
        for k in range(8):
            spill_ref[o + k] = cb[k]
        spill_ref[o + 8] = a[g]
        spill_ref[o + 9] = b[g]
        d = [[sub(o + k, r) if r >= k else None for k in range(8)] for r in range(8)]
        ar = [sub(o + 8, k) for k in range(8)]
        br = [sub(o + 9, k) for k in range(8)]
        rs = [None] * 8
        l = [[None] * 8 for _ in range(8)]

        def apply(k):
            ar[k] = ar[k] * rs[k]
            br[k] = br[k] * rs[k]
            if even:
                cc[k] = cc[k] * rs[k]
            for m in range(k + 1, 8):
                ar[m] = ar[m] - l[m][k] * ar[k]
                br[m] = br[m] - l[m][k] * br[k]
                if even:
                    cc[m] = cc[m] - l[m][k] * cc[k]
            if even:
                a[g + 1] = a[g + 1] - cc[k] * ar[k]
                b[g + 1] = b[g + 1] - cc[k] * br[k]
                spill_ref[o + 16 + k] = cc[k]
                for q in range(8):
                    nb[q] = nb[q] - cc[k] * sub(o + 16 + k, q)

        for k in range(0, 8, 2):
            r0 = lax.rsqrt(d[k][k])
            det = d[k][k] * d[k + 1][k + 1] - d[k + 1][k] * d[k + 1][k]
            rs[k] = r0
            rs[k + 1] = lax.rsqrt(det) * (d[k][k] * r0)
            for m in range(k + 1, 8):
                l[m][k] = d[m][k] * r0
            for m in range(k + 2, 8):
                l[m][k + 1] = (d[m][k + 1] - l[m][k] * l[k + 1][k]) * rs[k + 1]
            for m in range(k + 2, 8):
                for j in range(k + 2, m + 1):
                    d[m][j] = (d[m][j] - l[m][k] * l[j][k]) - l[m][k + 1] * l[j][k + 1]
            apply(k)
            apply(k + 1)
        if even:
            held = nb
        v = br[7]
        for k in range(7):
            v = jnp.where(ri == k, br[k], v)
        out.append(v)
        if filler is not None:
            next(filler, None)
        first = g + 2 if even else g + 1
        if first < 16:
            z = [None] * 8
            y = [None] * 8
            for k in range(7, -1, -1):
                zz = ar[k]
                yy = br[k]
                for m in range(7, k, -1):
                    zz = zz - l[m][k] * z[m]
                    yy = yy - l[m][k] * y[m]
                z[k] = zz * rs[k]
                y[k] = yy * rs[k]
            for i in range(first, 16):
                ai = a[i]
                bi = b[i]
                for k in range(8):
                    c = lane(a[i], 8 * g + k)
                    ai = ai - c * z[k]
                    bi = bi - c * y[k]
                a[i] = ai
                b[i] = bi
    return jnp.concatenate(out, axis=0)


def invert_panel(a_ref, w_ref, spill_ref, fillers):
    def rest(s, w_left, w_right, near):
        e = s + 128
        n = e + 128
        low = near
        if n < NB:
            far = split2(nt(left4(split2(a_ref[n:NB, s:e])), w_right))
            low = [jnp.concatenate([p, q], axis=0) for p, q in zip(near, far)]
            yield
            right = right4(low, 1)
            for i in range(n, NB, 128):
                left = left4([p[i - e : i - e + 128, :] for p in low])
                a_ref[i : i + 128, e : i + 128] = a_ref[i : i + 128, e : i + 128] - nt(
                    left, right[: i + 128 - e, :]
                )
                yield
        if s > 0:
            w_ref[s:e, 0:s] = nn(w_left, right4(split2(w_ref[s:e, 0:s]), 0))
            yield
        if e < NB:
            w_ref[e:NB, 0:e] = w_ref[e:NB, 0:e] - nn(
                left4(low), right4(split2(w_ref[s:e, 0:e]), 0)
            )
            yield

    w_ref[...] = jnp.zeros((NB, NB), f32)
    block = a_ref[0:128, 0:128]
    pending = ()
    for s in range(0, NB, 128):
        e = s + 128
        filler = itertools.chain(pending, fillers[s // 128])
        w = invert_factor(block, spill_ref, filler)
        for _ in filler:
            pass
        w_ref[s:e, s:e] = w
        pieces = split2(w)
        w_right = right4(pieces, 1)
        near = None
        if e < NB:
            near = split2(nt(left4(split2(a_ref[e : e + 128, s:e])), w_right))
            block = a_ref[e : e + 128, e : e + 128] - nt(left4(near), right4(near, 1))
        pending = rest(s, left4(pieces), w_right, near)
    for _ in pending:
        pass


def times_inverse(left, pieces):
    half = NB // 2
    lp = split2(left)
    top = nt(left3([p[:, :half] for p in lp]), right3([p[:half, :half] for p in pieces]))
    bottom = nt(left3(lp), right3([p[half:, :] for p in pieces]))
    return jnp.concatenate([top, bottom], axis=1)


def factor_kernel(
    lead_ref, scale_ref,
    right_ref, norm_ref, lead_noise_ref, w_ref, p21_ref, slots_ref, noises_ref, next_ref,
    a_ref, inv_ref, spill_ref,
):
    scale = scale_ref[...]
    slot_table, noise_table = read_tables(lead_ref)

    def lead_rows(panel):
        slots = spread_rows(slot_table, panel)
        noises = spread_rows(noise_table, panel)
        rows = []
        for c in range(4):
            hot = one_hot(slots[c : c + 1, :])
            at = panel * NB + c * 128
            rows.append(nn(hot, lead_ref[:, c, 8 * panel : 8 * panel + 8, :].reshape(128, F)))
            lead_noise_ref[at : at + 128, :] = place_noise(hot, noises[c : c + 1, :])
        rows = jnp.concatenate(rows, axis=0).astype(bf16)
        right_ref[panel], norm_ref[panel] = right_operand(rows, scale)
        return left_operand(rows, scale)

    a_ref[0] = add_diagonal(
        kernel_values(*lead_rows(0), right_ref[0], norm_ref[0]), lead_noise_ref[:NB, :]
    )

    def rest():
        left = lead_rows(1)
        yield
        a_ref[1] = kernel_values(*left, right_ref[0], norm_ref[0])
        yield
        a_ref[2] = add_diagonal(
            kernel_values(*left, right_ref[1], norm_ref[1]), lead_noise_ref[NB:, :]
        )
        yield
        blocks = positions()
        for kind in range(3):
            slots_ref[kind] = spread_rows(slot_table, blocks[2 * kind])
            noises_ref[kind] = spread_rows(noise_table, blocks[2 * kind])
            yield

    half = NB // 2

    def first_half():
        below = split2(a_ref[1, :, :half])
        p21 = nt(left3(below), right3(split2(inv_ref[:half, :half]))).astype(bf16)
        p21_ref[:, :half] = p21
        yield
        next_ref[...] = a_ref[2] - nt(p21, p21)
        yield

    invert_panel(a_ref.at[0], inv_ref, spill_ref, (rest(), (), first_half(), ()))
    pieces = split2(inv_ref[...])
    for i in range(2):
        w_ref[i] = pieces[i]
    p21 = nt(left3(split2(a_ref[1])), right3([p[half:, :] for p in pieces])).astype(bf16)
    p21_ref[:, half:] = p21
    next_ref[...] = next_ref[...] - nt(p21, p21)


def second_panel(
    bulk_ref, slots_ref, noises_ref, scale_ref, right_ref, norm_ref, lead_noise_ref,
    w_ref, next_ref, rows_ref, row_noise_ref, p_ref, w2_ref, a_ref, inv_ref, spill_ref,
):
    a_ref[...] = next_ref[...]
    scale = scale_ref[...]
    half = NB // 2
    blocks = positions()

    def units():
        for tile in range(6):
            at = slice(tile * NB, (tile + 1) * NB)
            rows = []
            for i in range(4):
                kind, c = divmod(tile * 4 + i, 8)
                hot = one_hot(slots_ref[kind, c : c + 1, :])
                rows.append(nn(hot, bulk_ref[:, c, 8 * kind : 8 * kind + 8, :].reshape(128, F)))
                if kind == 0:
                    row_noise_ref[c * 128 : c * 128 + 128, :] = place_noise(
                        hot, noises_ref[kind, c : c + 1, :]
                    )
            rows = jnp.concatenate(rows, axis=0).astype(bf16)
            rows_ref[at, :] = rows
            yield
            value = kernel_values(*left_operand(rows, scale), right_ref[0], norm_ref[0])
            lead = jnp.where(blocks[tile] == 0, lead_noise_ref[:NB, :], 0.0)
            pieces = split2(add_diagonal(value, lead))
            yield
            top = nt(
                left3([p[:, :half] for p in pieces]),
                right3([w_ref[i, :half, :half] for i in range(2)]),
            )
            p_ref[at, :half] = top.astype(bf16)
            yield
            bottom = nt(left3(pieces), right3([w_ref[i, half:, :] for i in range(2)]))
            p_ref[at, half:NB] = bottom.astype(bf16)
            yield

    work = units()
    invert_panel(a_ref, inv_ref, spill_ref, [itertools.islice(work, 6) for _ in range(4)])
    for _ in work:
        pass
    pieces = split2(inv_ref[...])
    for i in range(2):
        w2_ref[i] = pieces[i]


def output_kernel(
    bulk_ref, slots_ref, noises_ref, scale_ref, lead_ref, lead_norm_ref, lead_noise_ref,
    w1_ref, p21_ref, next_ref, out_ref, rows_ref, row_noise_ref, p_ref, w_ref, a_ref, inv_ref,
    spill_ref, left_ref, left_norm_ref, right_ref, right_norm_ref,
):
    @pl.when(pl.program_id(0) == 0)
    def _():
        second_panel(
            bulk_ref, slots_ref, noises_ref, scale_ref, lead_ref, lead_norm_ref, lead_noise_ref,
            w1_ref, next_ref, rows_ref, row_noise_ref, p_ref, w_ref, a_ref, inv_ref, spill_ref,
        )

    step = pl.program_id(0) - 1
    blocks = positions()
    tall = 2 * NB

    @pl.when((step >= 0) & (step < 3))
    def _():
        pair = [pick(blocks[i::2], step) for i in range(2)]
        at = pl.multiple_of(step * tall, tall)
        rows = rows_ref[pl.ds(at, tall), :]
        scale = scale_ref[...]
        left, left_norm = left_operand(rows, scale)

        @pl.when(step == 0)
        def _():
            left_ref[...] = left
            left_norm_ref[...] = left_norm

        @pl.when(step >= 1)
        def _():
            right, norm = right_operand(rows, scale)
            for i in range(2):
                right_ref[2 * step - 2 + i] = right[i * NB : (i + 1) * NB, :]
                right_norm_ref[2 * step - 2 + i] = norm[:, i * NB : (i + 1) * NB]

        value = kernel_values(left, left_norm, lead_ref[1], lead_norm_ref[1])
        noise = lead_noise_ref[NB:, :]
        value = jnp.concatenate(
            [
                add_diagonal(value[i * NB : (i + 1) * NB, :], jnp.where(pair[i] == 1, noise, 0.0))
                for i in range(2)
            ],
            axis=0,
        )
        p1 = p_ref[pl.ds(at, tall), :NB]
        second = value - nt(p1, p21_ref[...])
        p2 = times_inverse(second, [w_ref[i] for i in range(2)])
        for i in range(2):
            kept = jnp.where(pair[i] >= 1, p2[i * NB : (i + 1) * NB, :], 0.0)
            p_ref[pl.ds(at + i * NB, NB), NB:] = kept.astype(bf16)

    @pl.when(step >= 3)
    def _():
        column = step - 3
        j = 2 * (column % 2) + column // 2
        col_block = pick(blocks[2:], j)

        @pl.when(col_block == 0)
        def _():
            out_ref[...] = p_ref[:tall, :NB]

        @pl.when(col_block == 1)
        def _():
            out_ref[...] = p_ref[:tall, NB:]

        @pl.when(col_block >= PANELS)
        def _():
            value = kernel_values(left_ref[...], left_norm_ref[...], right_ref[j], right_norm_ref[j])
            at = pl.multiple_of((2 + j) * NB, NB)
            value = value - nt(p_ref[:tall, :], p_ref[pl.ds(at, NB), :])
            for i in range(2):
                noise = row_noise_ref[i * NB : (i + 1) * NB, :]
                noise = jnp.where(blocks[i] == col_block, noise, 0.0)
                half = add_diagonal(value[i * NB : (i + 1) * NB, :], noise)
                half = jnp.where(blocks[i] >= PANELS, half, 0.0)
                out_ref[i * NB : (i + 1) * NB, :] = half.astype(bf16)


VMEM = pl.BlockSpec(memory_space=pltpu.VMEM)
SMEM = pl.BlockSpec(memory_space=pltpu.SMEM)
PARAMS = pltpu.CompilerParams(vmem_limit_bytes=56 * 1024 * 1024)


def body(features, noise, owner_slot, inv_length):
    nrows = lax.axis_size("row")
    ncols = lax.axis_size("col")
    here = features.shape[0]
    count = nrows * ncols
    scale = inv_length.reshape(1, F)

    arranged, lead_send = pl.pallas_call(
        pack_kernel,
        out_shape=(
            jax.ShapeDtypeStruct((here, F), bf16),
            jax.ShapeDtypeStruct((count, 24, F), bf16),
        ),
        in_specs=[VMEM] * 3,
        out_specs=(VMEM, VMEM),
        name="pack",
    )(features, noise.reshape(1, here), owner_slot.reshape(1, here))
    lead = lax.all_to_all(lead_send, ("row", "col"), 0, 0, tiled=True)

    groups = arranged.reshape(nrows, 8, F)
    to_row = jnp.broadcast_to(groups[:, None], (nrows, ncols, 8, F))
    to_col = jnp.broadcast_to(groups.reshape(1, 2, ncols, 8, F), (nrows, 2, ncols, 8, F))
    bulk_send = jnp.concatenate([to_row, to_col[:, 0], to_col[:, 1]], axis=2)
    bulk_send = bulk_send.reshape(count, 24, F)
    bulk_send, lead = lax.optimization_barrier((bulk_send, lead))
    bulk = lax.all_to_all(bulk_send, ("row", "col"), 0, 0, tiled=True)

    right, norm, lead_noise, w1, p21, slots, noises, trailing = pl.pallas_call(
        factor_kernel,
        out_shape=(
            jax.ShapeDtypeStruct((PANELS, NB, 2 * F), bf16),
            jax.ShapeDtypeStruct((PANELS, 8, NB), f32),
            jax.ShapeDtypeStruct((PANELS * NB, 128), f32),
            jax.ShapeDtypeStruct((2, NB, NB), bf16),
            jax.ShapeDtypeStruct((NB, NB), bf16),
            jax.ShapeDtypeStruct((3, 8, here), f32),
            jax.ShapeDtypeStruct((3, 8, here), f32),
            jax.ShapeDtypeStruct((NB, NB), f32),
        ),
        in_specs=[VMEM] * 2,
        out_specs=(VMEM,) * 8,
        scratch_shapes=[
            pltpu.VMEM((3, NB, NB), f32),
            pltpu.VMEM((NB, NB), f32),
            pltpu.VMEM((64, 8, 128), f32),
        ],
        compiler_params=PARAMS,
        name="first_panel",
    )(lead.reshape(nrows, ncols, 24, F), scale)

    return pl.pallas_call(
        output_kernel,
        grid=(8,),
        in_specs=[VMEM] * 10,
        out_specs=pl.BlockSpec((2 * NB, NB), lambda i: (0, jnp.maximum(i - 4, 0))),
        scratch_shapes=[
            pltpu.VMEM((6 * NB, F), bf16),
            pltpu.VMEM((2 * NB, 128), f32),
            pltpu.VMEM((6 * NB, PANELS * NB), bf16),
            pltpu.VMEM((2, NB, NB), bf16),
            pltpu.VMEM((NB, NB), f32),
            pltpu.VMEM((NB, NB), f32),
            pltpu.VMEM((64, 8, 128), f32),
            pltpu.VMEM((2 * NB, 2 * F), bf16),
            pltpu.VMEM((2 * NB, 128), f32),
            pltpu.VMEM((4, NB, 2 * F), bf16),
            pltpu.VMEM((4, 8, NB), f32),
        ],
        out_shape=jax.ShapeDtypeStruct((2 * NB, 4 * NB), bf16),
        compiler_params=PARAMS,
        name="output",
    )(
        bulk.reshape(nrows, ncols, 24, F), slots, noises, scale, right, norm, lead_noise, w1,
        p21, trailing,
    )


def solution(mesh):
    in_specs = (P(("row", "col"), None), P(("row", "col")), P(("row", "col")), P())
    out_specs = P("row", "col")
    return jax.shard_map(body, mesh=mesh, in_specs=in_specs, out_specs=out_specs, check_vma=False)
```

```python
import itertools

import jax
import jax.numpy as jnp
from jax import lax
from jax.experimental import pallas as pl
from jax.experimental.pallas import tpu as pltpu
from jax.sharding import PartitionSpec as P

NB = 512
PANELS = 2
F = 128
f32 = jnp.float32
bf16 = jnp.bfloat16


def split2(x):
    h = x.astype(bf16)
    return h, (x - h.astype(f32)).astype(bf16)


def left4(pieces):
    h, m = pieces
    return jnp.concatenate([h, h, m, m], axis=1)


def right4(pieces, axis):
    h, m = pieces
    return jnp.concatenate([h, m, h, m], axis=axis)


def left3(pieces):
    h, m = pieces
    return jnp.concatenate([h, h, m], axis=1)


def right3(pieces):
    h, m = pieces
    return jnp.concatenate([h, m, h], axis=1)


def nt(x, y):
    return lax.dot_general(x, y, (((1,), (1,)), ((), ())), preferred_element_type=f32)


def nn(x, y):
    return lax.dot_general(x, y, (((1,), (0,)), ((), ())), preferred_element_type=f32)


def iota(shape, dim):
    return lax.broadcasted_iota(jnp.int32, shape, dim)


def pack_kernel(feat_ref, noise_ref, slot_ref, sorted_ref, lead_ref):
    n = feat_ref.shape[0]
    eye = iota((n, n), 0) == iota((n, n), 1)
    row = slot_ref[...].astype(f32)
    col = jnp.sum(jnp.where(eye, row, 0.0), axis=1, keepdims=True)
    noise = noise_ref[...].astype(bf16).astype(f32)
    noise = jnp.sum(jnp.where(eye, noise, 0.0), axis=1, keepdims=True)
    local = (slot_ref[...] % n).astype(f32)
    local = jnp.sum(jnp.where(eye, local, 0.0), axis=1, keepdims=True)
    rank_col = jnp.sum((row < col).astype(f32), axis=1, keepdims=True)
    rank_row = jnp.sum((col < row).astype(f32), axis=0, keepdims=True)
    arranged = nn((iota((n, n), 0).astype(f32) == rank_row).astype(bf16), feat_ref[...].astype(bf16))
    sorted_ref[...] = arranged.astype(bf16)
    back = rank_col == iota((n, n), 1).astype(f32)
    slots = jnp.sum(jnp.where(back, local, 0.0), axis=0, keepdims=True)
    noises = jnp.sum(jnp.where(back, noise, 0.0), axis=0, keepdims=True)
    c = lax.axis_index("col").astype(jnp.int32)
    which = iota((8, n), 0)
    extra = jnp.where(which == c, slots, jnp.where((which + 4) % 8 == c, noises, 0.0))
    block = jnp.concatenate([arranged[:16], extra], axis=0).astype(bf16)
    lead_ref[...] = jnp.broadcast_to(block[None], lead_ref.shape)


def spread_rows(table, target):
    n = table.shape[0]
    lane = iota((n, n), 1)
    mine = jnp.where(lane // 8 == target, table, jnp.zeros_like(table))
    comb = (iota((n, n), 0) % 8 == iota((n, n), 1) % 8).astype(bf16)
    spread = nn(mine, comb).reshape(n // 8, 8, n)
    take = iota((n // 8, 8, n), 2) // 8 == iota((n // 8, 8, n), 0)
    return jnp.sum(jnp.where(take, spread, 0.0), axis=0)


def read_tables(lead_ref):
    nrows = lead_ref.shape[0]
    slots, noises = [], []
    low = iota((8, 128), 0) < 4
    for r in range(nrows):
        parts = [lead_ref[r, c, 16:24, :].astype(f32) for c in range(8)]
        first = (parts[0] + parts[1]) + (parts[2] + parts[3])
        last = (parts[4] + parts[5]) + (parts[6] + parts[7])
        slots.append(jnp.where(low, first, last))
        other = jnp.where(low, last, first)
        noises.append(jnp.concatenate([other[4:], other[:4]], axis=0))
    return (
        jnp.concatenate(slots, axis=0).astype(bf16),
        jnp.concatenate(noises, axis=0).astype(bf16),
    )


def positions():
    nrows = lax.axis_size("row")
    ncols = lax.axis_size("col")
    r = lax.axis_index("row").astype(jnp.int32)
    c = lax.axis_index("col").astype(jnp.int32)
    return [r, r + nrows, c, c + 2 * ncols, c + ncols, c + 3 * ncols]


def pick(values, index):
    out = values[0]
    for i, v in enumerate(values[1:]):
        out = jnp.where(index == i + 1, v, out)
    return out


def one_hot(slots):
    n = slots.shape[1]
    return (iota((n, n), 0).astype(f32) == slots).astype(bf16)


def place_noise(hot, noises):
    return nt(jnp.broadcast_to(noises.astype(bf16), (8, hot.shape[1])), hot)


def norm_pieces(rows, scale):
    x = rows.astype(f32)
    return jnp.concatenate(split2(-0.5 * (x * x * scale)), axis=1)


def left_operand(rows, scale):
    norm = nn(norm_pieces(rows, scale), jnp.ones((2 * F, 128), bf16))
    return jnp.concatenate([rows, rows], axis=1), norm


def right_operand(rows, scale):
    norm = nt(jnp.ones((8, 2 * F), bf16), norm_pieces(rows, scale))
    return jnp.concatenate(split2(rows.astype(f32) * scale), axis=1), norm


def kernel_values(left, left_norm, right, right_norm):
    wide = jnp.concatenate([left_norm] * (right.shape[0] // 128), axis=1)
    return jnp.exp(nt(left, right) + wide + right_norm[0:1, :])


def add_diagonal(value, noise, start=0):
    n, width = value.shape
    eye = iota((128, 128), 0) == iota((128, 128), 1)
    bands = []
    for i in range(0, n, 128):
        band = value[i : i + 128, :]
        at = start + i
        square = band[:, at : at + 128] + jnp.where(eye, noise[0:1, i : i + 128], 0.0)
        parts = [band[:, :at], square, band[:, at + 128 :]]
        bands.append(jnp.concatenate([p for p in parts if p.shape[1]], axis=1))
    return jnp.concatenate(bands, axis=0)


def lane(x, j):
    return jnp.broadcast_to(x[:, j : j + 1], (8, 128))


def invert_factor(block, spill_ref, filler=None):
    def sub(q, k):
        return jnp.broadcast_to(spill_ref[q, k : k + 1, :], (8, 128))

    ri = iota((8, 128), 0)
    ci = iota((8, 128), 1)
    a = [block[8 * i : 8 * i + 8, :] for i in range(16)]
    b = [(ri + 8 * i == ci).astype(f32) for i in range(16)]
    out = []
    held = None
    for g in range(16):
        even = g % 2 == 0
        o = 32 * (g % 2)
        cb = [lane(a[g], 8 * g + k) for k in range(8)] if even else held
        cc = [lane(a[g + 1], 8 * g + k) for k in range(8)] if even else None
        nb = [lane(a[g + 1], 8 * g + 8 + k) for k in range(8)] if even else None
        for k in range(8):
            spill_ref[o + k] = cb[k]
        spill_ref[o + 8] = a[g]
        spill_ref[o + 9] = b[g]
        d = [[sub(o + k, r) if r >= k else None for k in range(8)] for r in range(8)]
        ar = [sub(o + 8, k) for k in range(8)]
        br = [sub(o + 9, k) for k in range(8)]
        rs = [None] * 8
        l = [[None] * 8 for _ in range(8)]

        def apply(k):
            ar[k] = ar[k] * rs[k]
            br[k] = br[k] * rs[k]
            if even:
                cc[k] = cc[k] * rs[k]
            for m in range(k + 1, 8):
                ar[m] = ar[m] - l[m][k] * ar[k]
                br[m] = br[m] - l[m][k] * br[k]
                if even:
                    cc[m] = cc[m] - l[m][k] * cc[k]
            if even:
                a[g + 1] = a[g + 1] - cc[k] * ar[k]
                b[g + 1] = b[g + 1] - cc[k] * br[k]
                spill_ref[o + 16 + k] = cc[k]
                for q in range(8):
                    nb[q] = nb[q] - cc[k] * sub(o + 16 + k, q)

        for k in range(0, 8, 2):
            r0 = lax.rsqrt(d[k][k])
            det = d[k][k] * d[k + 1][k + 1] - d[k + 1][k] * d[k + 1][k]
            rs[k] = r0
            rs[k + 1] = lax.rsqrt(det) * (d[k][k] * r0)
            for m in range(k + 1, 8):
                l[m][k] = d[m][k] * r0
            for m in range(k + 2, 8):
                l[m][k + 1] = (d[m][k + 1] - l[m][k] * l[k + 1][k]) * rs[k + 1]
            for m in range(k + 2, 8):
                for j in range(k + 2, m + 1):
                    d[m][j] = (d[m][j] - l[m][k] * l[j][k]) - l[m][k + 1] * l[j][k + 1]
            apply(k)
            apply(k + 1)
        if even:
            held = nb
        v = br[7]
        for k in range(7):
            v = jnp.where(ri == k, br[k], v)
        out.append(v)
        if filler is not None:
            next(filler, None)
        first = g + 2 if even else g + 1
        if first < 16:
            z = [None] * 8
            y = [None] * 8
            for k in range(7, -1, -1):
                zz = ar[k]
                yy = br[k]
                for m in range(7, k, -1):
                    zz = zz - l[m][k] * z[m]
                    yy = yy - l[m][k] * y[m]
                z[k] = zz * rs[k]
                y[k] = yy * rs[k]
            for i in range(first, 16):
                ai = a[i]
                bi = b[i]
                for k in range(8):
                    c = lane(a[i], 8 * g + k)
                    ai = ai - c * z[k]
                    bi = bi - c * y[k]
                a[i] = ai
                b[i] = bi
    return jnp.concatenate(out, axis=0)


def invert_panel(a_ref, w_ref, spill_ref, fillers):
    def rest(s, w_left, w_right, near):
        e = s + 128
        n = e + 128
        low = near
        if n < NB:
            far = split2(nt(left4(split2(a_ref[n:NB, s:e])), w_right))
            low = [jnp.concatenate([p, q], axis=0) for p, q in zip(near, far)]
            yield
            right = right4(low, 1)
            for i in range(n, NB, 128):
                left = left4([p[i - e : i - e + 128, :] for p in low])
                a_ref[i : i + 128, e : i + 128] = a_ref[i : i + 128, e : i + 128] - nt(
                    left, right[: i + 128 - e, :]
                )
                yield
        if s > 0:
            w_ref[s:e, 0:s] = nn(w_left, right4(split2(w_ref[s:e, 0:s]), 0))
            yield
        if e < NB:
            w_ref[e:NB, 0:e] = w_ref[e:NB, 0:e] - nn(
                left4(low), right4(split2(w_ref[s:e, 0:e]), 0)
            )
            yield

    w_ref[...] = jnp.zeros((NB, NB), f32)
    block = a_ref[0:128, 0:128]
    pending = ()
    for s in range(0, NB, 128):
        e = s + 128
        filler = itertools.chain(pending, fillers[s // 128])
        w = invert_factor(block, spill_ref, filler)
        for _ in filler:
            pass
        w_ref[s:e, s:e] = w
        pieces = split2(w)
        w_right = right4(pieces, 1)
        near = None
        if e < NB:
            near = split2(nt(left4(split2(a_ref[e : e + 128, s:e])), w_right))
            block = a_ref[e : e + 128, e : e + 128] - nt(left4(near), right4(near, 1))
        pending = rest(s, left4(pieces), w_right, near)
    for _ in pending:
        pass


def times_inverse(left, pieces):
    half = NB // 2
    lp = split2(left)
    top = nt(left3([p[:, :half] for p in lp]), right3([p[:half, :half] for p in pieces]))
    bottom = nt(left3(lp), right3([p[half:, :] for p in pieces]))
    return jnp.concatenate([top, bottom], axis=1)


def factor_kernel(
    lead_ref, scale_ref,
    right_ref, norm_ref, lead_noise_ref, w_ref, p21_ref, slots_ref, noises_ref, next_ref,
    a_ref, inv_ref, spill_ref,
):
    scale = scale_ref[...]
    slot_table, noise_table = read_tables(lead_ref)

    def lead_rows(panel):
        slots = spread_rows(slot_table, panel)
        noises = spread_rows(noise_table, panel)
        rows = []
        for c in range(4):
            hot = one_hot(slots[c : c + 1, :])
            at = panel * NB + c * 128
            rows.append(nn(hot, lead_ref[:, c, 8 * panel : 8 * panel + 8, :].reshape(128, F)))
            lead_noise_ref[:, at : at + 128] = place_noise(hot, noises[c : c + 1, :])
        rows = jnp.concatenate(rows, axis=0).astype(bf16)
        right_ref[panel], norm_ref[panel] = right_operand(rows, scale)
        return left_operand(rows, scale)

    a_ref[0] = add_diagonal(
        kernel_values(*lead_rows(0), right_ref[0], norm_ref[0]), lead_noise_ref[:, :NB]
    )

    def rest():
        left = lead_rows(1)
        yield
        a_ref[1] = kernel_values(*left, right_ref[0], norm_ref[0])
        yield
        a_ref[2] = add_diagonal(
            kernel_values(*left, right_ref[1], norm_ref[1]), lead_noise_ref[:, NB:]
        )
        yield
        blocks = positions()
        for kind in range(3):
            slots_ref[kind] = spread_rows(slot_table, blocks[2 * kind])
            noises_ref[kind] = spread_rows(noise_table, blocks[2 * kind])
            yield

    half = NB // 2

    def first_half():
        below = split2(a_ref[1, :, :half])
        p21 = nt(left3(below), right3(split2(inv_ref[:half, :half]))).astype(bf16)
        p21_ref[:, :half] = p21
        yield
        next_ref[...] = a_ref[2] - nt(p21, p21)
        yield

    invert_panel(a_ref.at[0], inv_ref, spill_ref, (rest(), (), first_half(), ()))
    pieces = split2(inv_ref[...])
    for i in range(2):
        w_ref[i] = pieces[i]
    p21 = nt(left3(split2(a_ref[1])), right3([p[half:, :] for p in pieces])).astype(bf16)
    p21_ref[:, half:] = p21
    next_ref[...] = next_ref[...] - nt(p21, p21)


def second_panel(
    bulk_ref, slots_ref, noises_ref, scale_ref, right_ref, norm_ref, lead_noise_ref,
    w_ref, next_ref, rows_ref, row_noise_ref, p_ref, w2_ref, a_ref, inv_ref, spill_ref,
):
    a_ref[...] = next_ref[...]
    scale = scale_ref[...]
    half = NB // 2
    blocks = positions()

    def units():
        for tile in range(6):
            at = slice(tile * NB, (tile + 1) * NB)
            rows = []
            for i in range(4):
                kind, c = divmod(tile * 4 + i, 8)
                hot = one_hot(slots_ref[kind, c : c + 1, :])
                rows.append(nn(hot, bulk_ref[:, c, 8 * kind : 8 * kind + 8, :].reshape(128, F)))
                if kind == 0:
                    row_noise_ref[:, c * 128 : c * 128 + 128] = place_noise(
                        hot, noises_ref[kind, c : c + 1, :]
                    )
            rows = jnp.concatenate(rows, axis=0).astype(bf16)
            rows_ref[at, :] = rows
            yield
            value = kernel_values(*left_operand(rows, scale), right_ref[0], norm_ref[0])
            lead = jnp.where(blocks[tile] == 0, lead_noise_ref[:, :NB], 0.0)
            pieces = split2(add_diagonal(value, lead))
            yield
            top = nt(
                left3([p[:, :half] for p in pieces]),
                right3([w_ref[i, :half, :half] for i in range(2)]),
            )
            p_ref[at, :half] = top.astype(bf16)
            yield
            bottom = nt(left3(pieces), right3([w_ref[i, half:, :] for i in range(2)]))
            p_ref[at, half:NB] = bottom.astype(bf16)
            yield

    work = units()
    invert_panel(a_ref, inv_ref, spill_ref, [itertools.islice(work, 6) for _ in range(4)])
    for _ in work:
        pass
    pieces = split2(inv_ref[...])
    for i in range(2):
        w2_ref[i] = pieces[i]


def output_kernel(
    bulk_ref, slots_ref, noises_ref, scale_ref, lead_ref, lead_norm_ref, lead_noise_ref,
    w1_ref, p21_ref, next_ref, out_ref, rows_ref, row_noise_ref, p_ref, w_ref, a_ref, inv_ref,
    spill_ref, left_ref, left_norm_ref, right_ref, right_norm_ref,
):
    @pl.when(pl.program_id(0) == 0)
    def _():
        second_panel(
            bulk_ref, slots_ref, noises_ref, scale_ref, lead_ref, lead_norm_ref, lead_noise_ref,
            w1_ref, next_ref, rows_ref, row_noise_ref, p_ref, w_ref, a_ref, inv_ref, spill_ref,
        )

    step = pl.program_id(0) - 1
    blocks = positions()
    tall = 2 * NB

    @pl.when((step >= 0) & (step < 3))
    def _():
        pair = [pick(blocks[i::2], step) for i in range(2)]
        at = pl.multiple_of(step * tall, tall)
        rows = rows_ref[pl.ds(at, tall), :]
        scale = scale_ref[...]
        left, left_norm = left_operand(rows, scale)

        @pl.when(step == 0)
        def _():
            left_ref[...] = left
            left_norm_ref[...] = left_norm

        @pl.when(step >= 1)
        def _():
            right, norm = right_operand(rows, scale)
            for i in range(2):
                right_ref[2 * step - 2 + i] = right[i * NB : (i + 1) * NB, :]
                right_norm_ref[2 * step - 2 + i] = norm[:, i * NB : (i + 1) * NB]

        value = kernel_values(left, left_norm, lead_ref[1], lead_norm_ref[1])
        noise = lead_noise_ref[:, NB:]
        value = jnp.concatenate(
            [
                add_diagonal(value[i * NB : (i + 1) * NB, :], jnp.where(pair[i] == 1, noise, 0.0))
                for i in range(2)
            ],
            axis=0,
        )
        p1 = p_ref[pl.ds(at, tall), :NB]
        second = value - nt(p1, p21_ref[...])
        p2 = times_inverse(second, [w_ref[i] for i in range(2)])
        for i in range(2):
            kept = jnp.where(pair[i] >= 1, p2[i * NB : (i + 1) * NB, :], 0.0)
            p_ref[pl.ds(at + i * NB, NB), NB:] = kept.astype(bf16)

    @pl.when(step >= 3)
    def _():
        column = step - 3
        j = 2 * (column % 2) + column // 2
        col_block = pick(blocks[2:], j)

        @pl.when(col_block == 0)
        def _():
            out_ref[...] = p_ref[:tall, :NB]

        @pl.when(col_block == 1)
        def _():
            out_ref[...] = p_ref[:tall, NB:]

        @pl.when(col_block >= PANELS)
        def _():
            value = kernel_values(left_ref[...], left_norm_ref[...], right_ref[j], right_norm_ref[j])
            at = pl.multiple_of((2 + j) * NB, NB)
            value = value - nt(p_ref[:tall, :], p_ref[pl.ds(at, NB), :])
            for i in range(2):
                noise = row_noise_ref[:, i * NB : (i + 1) * NB]
                noise = jnp.where(blocks[i] == col_block, noise, 0.0)
                half = add_diagonal(value[i * NB : (i + 1) * NB, :], noise)
                half = jnp.where(blocks[i] >= PANELS, half, 0.0)
                out_ref[i * NB : (i + 1) * NB, :] = half.astype(bf16)


VMEM = pl.BlockSpec(memory_space=pltpu.VMEM)
SMEM = pl.BlockSpec(memory_space=pltpu.SMEM)
PARAMS = pltpu.CompilerParams(vmem_limit_bytes=44 * 1024 * 1024)


def body(features, noise, owner_slot, inv_length):
    nrows = lax.axis_size("row")
    ncols = lax.axis_size("col")
    here = features.shape[0]
    count = nrows * ncols
    scale = inv_length.reshape(1, F)

    arranged, lead_send = pl.pallas_call(
        pack_kernel,
        out_shape=(
            jax.ShapeDtypeStruct((here, F), bf16),
            jax.ShapeDtypeStruct((count, 24, F), bf16),
        ),
        in_specs=[VMEM] * 3,
        out_specs=(VMEM, VMEM),
        name="pack",
    )(features, noise.reshape(1, here), owner_slot.reshape(1, here))
    lead = lax.all_to_all(lead_send, ("row", "col"), 0, 0, tiled=True)

    groups = arranged.reshape(nrows, 8, F)
    to_row = jnp.broadcast_to(groups[:, None], (nrows, ncols, 8, F))
    to_col = jnp.broadcast_to(groups.reshape(1, 2, ncols, 8, F), (nrows, 2, ncols, 8, F))
    bulk_send = jnp.concatenate([to_row, to_col[:, 0], to_col[:, 1]], axis=2)
    bulk_send = bulk_send.reshape(count, 24, F)
    bulk_send, lead = lax.optimization_barrier((bulk_send, lead))
    bulk = lax.all_to_all(bulk_send, ("row", "col"), 0, 0, tiled=True)

    lead = pltpu.with_memory_space_constraint(lead.reshape(nrows, ncols, 24, F), pltpu.VMEM)
    right, norm, lead_noise, w1, p21, slots, noises, trailing = pl.pallas_call(
        factor_kernel,
        out_shape=(
            pltpu.VMEM((PANELS, NB, 2 * F), bf16),
            pltpu.VMEM((PANELS, 8, NB), f32),
            pltpu.VMEM((8, PANELS * NB), f32),
            jax.ShapeDtypeStruct((2, NB, NB), bf16),
            jax.ShapeDtypeStruct((NB, NB), bf16),
            pltpu.VMEM((3, 8, here), f32),
            pltpu.VMEM((3, 8, here), f32),
            jax.ShapeDtypeStruct((NB, NB), f32),
        ),
        in_specs=[VMEM] * 2,
        out_specs=(VMEM,) * 8,
        scratch_shapes=[
            pltpu.VMEM((3, NB, NB), f32),
            pltpu.VMEM((NB, NB), f32),
            pltpu.VMEM((64, 8, 128), f32),
        ],
        compiler_params=PARAMS,
        name="first_panel",
    )(lead, scale)

    keep = lambda x: pltpu.with_memory_space_constraint(x, pltpu.VMEM)
    bulk = keep(bulk.reshape(nrows, ncols, 24, F))
    slots, noises, right, norm, lead_noise = map(
        keep, (slots, noises, right, norm, lead_noise)
    )
    return pl.pallas_call(
        output_kernel,
        grid=(8,),
        in_specs=[VMEM] * 10,
        out_specs=pl.BlockSpec((2 * NB, NB), lambda i: (0, jnp.maximum(i - 4, 0))),
        scratch_shapes=[
            pltpu.VMEM((6 * NB, F), bf16),
            pltpu.VMEM((8, 2 * NB), f32),
            pltpu.VMEM((6 * NB, PANELS * NB), bf16),
            pltpu.VMEM((2, NB, NB), bf16),
            pltpu.VMEM((NB, NB), f32),
            pltpu.VMEM((NB, NB), f32),
            pltpu.VMEM((64, 8, 128), f32),
            pltpu.VMEM((2 * NB, 2 * F), bf16),
            pltpu.VMEM((2 * NB, 128), f32),
            pltpu.VMEM((4, NB, 2 * F), bf16),
            pltpu.VMEM((4, 8, NB), f32),
        ],
        out_shape=jax.ShapeDtypeStruct((2 * NB, 4 * NB), bf16),
        compiler_params=PARAMS,
        name="output",
    )(
        bulk, slots, noises, scale, right, norm, lead_noise, w1, p21, trailing
    )


def solution(mesh):
    in_specs = (P(("row", "col"), None), P(("row", "col")), P(("row", "col")), P())
    out_specs = P("row", "col")
    return jax.shard_map(body, mesh=mesh, in_specs=in_specs, out_specs=out_specs, check_vma=False)
```
